512 devices in a mesh: band: 128 (over z, x, core), chan: 4 (over y).
Axes of the slice: x: 4, y: 4, z: 16, core: 2. Of those that a mesh axis runs over, the one named last changes fastest.
Arguments:
- features: bfloat16 [384, 256, 128], P('chan', 'band'), may hold values from -6 to 6
- h_kernel: float32 [384, 47], P('chan'), may hold values from -0.875 to 0.875
- v_kernel: float32 [384, 47], P('chan'), may hold values from -0.875 to 0.875
- h_kernel_avg: float32 [384, 47], P('chan'), may hold values from -0.875 to 0.875
- v_kernel_avg: float32 [384, 47], P('chan'), may hold values from -0.875 to 0.875
- norm_gain: float32 [384], replicated, may hold values from 0.1 to 1.9
- w_in: bfloat16 [384, 1536], replicated, may hold values from -0.3125 to 0.3125
- w_out: bfloat16 [1536, 384], replicated, may hold values from -0.15625 to 0.15625
- cotangent: bfloat16 [384, 256, 128], P('chan', 'band'), may hold values from -6 to 6
- tissue: int32 [256, 128], P('band'), may hold values 0 or 1
Outputs:
- block_out: bfloat16 [384, 256, 128], P('chan', 'band')
- h_kernel_new: float32 [384, 47], P('chan')
- v_kernel_new: float32 [384, 47], P('chan')
- h_kernel_swa: float32 [384, 47], P('chan')
- v_kernel_swa: float32 [384, 47], P('chan')
The draws below stay inside these ranges and needn't reach their ends.
All inputs are finite; a program needn't handle non-finite values. No bound on the sum of `tissue` on one device may be relied on, other than what follows from the above.
Results may differ from the reference program's by a relative error of at most 0.0063.
Values may be sent and summed in bfloat16 or wider, within the bound.
A program may use at most 64 MiB of HBM per device.

```python
import math
import jax
import jax.numpy as jnp
from jax import lax

C = 384
HID = 1536
K = 47
AVERAGED = 4
H = 256
W = 128
N_BAND = 128


def set_ends(values, own_key, smallest, high):
    index_at = [jax.random.randint(jax.random.fold_in(own_key, axis), (), 0, length) for axis, length in enumerate(values.shape)]
    main_axis = values.shape.index(max(values.shape))
    next_to = index_at[:main_axis] + [(index_at[main_axis] + 1) % values.shape[main_axis]] + index_at[main_axis + 1:]
    return values.at[tuple(index_at)].set(smallest).at[tuple(next_to)].set(high)


def levels(own_key, extent, shards, smallest, top_value):
    level = 1.0
    for dim, blocks in shards:
        draws = jax.random.uniform(jax.random.fold_in(jax.random.fold_in(own_key, 6), dim), (blocks,), jnp.float32, smallest / len(shards), top_value / len(shards))
        level = level * jnp.repeat(jnp.exp(draws), extent[dim] // blocks).reshape((-1,) + (1,) * (len(extent) - 1 - dim))
    return level


def gaussian(key, extent, spread, limit, pieces=(), kind=jnp.bfloat16):
    loudness = levels(key, extent, pieces, -0.22, 0.18) if pieces else 1.0
    entries = jax.random.normal(key, extent, jnp.float32) * spread * loudness
    return jnp.minimum(jnp.maximum(entries, -limit), limit).astype(kind)


def setup_inputs(seed: int = 0) -> dict:
    key_list = jax.random.split(jax.random.key(seed), 11)
    return {
        "features": gaussian(key_list[0], (C, H, W), 1.0, 6.0, ((0, 4), (1, 128))),
        "h_kernel": gaussian(key_list[1], (C, K), K ** -0.5, 0.875, ((0, 4),), jnp.float32),
        "v_kernel": gaussian(key_list[2], (C, K), K ** -0.5, 0.875, ((0, 4),), jnp.float32),
        "h_kernel_avg": gaussian(key_list[3], (C, K), K ** -0.5, 0.875, ((0, 4),), jnp.float32),
        "v_kernel_avg": gaussian(key_list[4], (C, K), K ** -0.5, 0.875, ((0, 4),), jnp.float32),
        "norm_gain": jnp.clip(1.0 + 0.18 * jax.random.normal(key_list[5], (C,), jnp.float32), 0.1, 1.9),
        "w_in": gaussian(key_list[6], (C, HID), C ** -0.5, 0.3125),
        "w_out": gaussian(key_list[7], (HID, C), HID ** -0.5, 0.15625),
        "cotangent": gaussian(key_list[8], (C, H, W), 1.0, 6.0, ((0, 4), (1, 128))),
        "tissue": set_ends((jax.random.randint(key_list[9], (H, W), 0, 5) < 3).astype(jnp.int32), jax.random.fold_in(key_list[9], 1), 0, 1),
    }


EPSILON = 1e-06
STEP_SIZE = 0.1
ROOT_HALF = math.sqrt(0.5)
INV_ROOT_TWO_PI = 1.0 / math.sqrt(2.0 * math.pi)

def depthwise(source, kernel, direction):
    radius = (kernel.shape[1] - 1) // 2
    if direction == 2:
        shaped = kernel[:, None, None, :]
        padding = ((0, 0), (radius, radius))
    else:
        shaped = kernel[:, None, :, None]
        padding = ((radius, radius), (0, 0))
    return lax.conv_general_dilated(source[None], shaped, (1, 1), padding, dimension_numbers=('NCHW', 'OIHW', 'NCHW'), feature_group_count=kernel.shape[0], preferred_element_type=jnp.float32)[0]

def tap_grad(source, upstream, direction, radius):
    widths = [(0, 0), (0, 0), (0, 0)]
    widths[direction] = (radius, radius)
    padded = jnp.pad(source.astype(jnp.float32), widths)
    upstream_wide = upstream.astype(jnp.float32)
    length = source.shape[direction]

    def one_tap(offset):
        window = lax.dynamic_slice_in_dim(padded, offset, length, direction)
        return lax.optimization_barrier(jnp.sum(window * upstream_wide, axis=(1, 2)))
    stacked = lax.map(one_tap, jnp.arange(2 * radius + 1, dtype=jnp.int32))
    return jnp.transpose(stacked)

def pointwise(values, upstream, norm_gain, w_in, w_out):
    widened = values.astype(jnp.float32)
    centred = widened - lax.optimization_barrier(jnp.mean(widened, axis=0, keepdims=True))
    inverse = lax.rsqrt(lax.optimization_barrier(jnp.mean(centred * centred, axis=0, keepdims=True)) + EPSILON)
    standard = centred * inverse
    normed = (standard * norm_gain[:, None]).astype(jnp.bfloat16)
    preact = jnp.dot(w_in.T, normed, preferred_element_type=jnp.float32)
    cumulative = 0.5 * (1.0 + lax.erf(preact * ROOT_HALF))
    activated = (preact * cumulative).astype(jnp.bfloat16)
    branch = jnp.dot(w_out.T, activated, preferred_element_type=jnp.float32).astype(jnp.bfloat16)
    grad_act = jnp.dot(w_out, upstream, preferred_element_type=jnp.float32)
    density = jnp.exp(-0.5 * preact * preact) * INV_ROOT_TWO_PI
    grad_pre = (grad_act * (cumulative + preact * density)).astype(jnp.bfloat16)
    grad_normed = jnp.dot(w_in, grad_pre, preferred_element_type=jnp.float32)
    scaled = grad_normed * norm_gain[:, None]
    grad_values = (scaled - lax.optimization_barrier(jnp.mean(scaled, axis=0, keepdims=True)) - standard * lax.optimization_barrier(jnp.mean(scaled * standard, axis=0, keepdims=True))) * inverse
    return (branch, grad_values.astype(jnp.bfloat16))

def reference(features, h_kernel, v_kernel, h_kernel_avg, v_kernel_avg, norm_gain, w_in, w_out, cotangent, tissue):
    radius = (h_kernel.shape[1] - 1) // 2
    h_half = h_kernel.astype(jnp.bfloat16)
    v_half = v_kernel.astype(jnp.bfloat16)
    smoothed = depthwise(features, h_half, 2).astype(jnp.bfloat16)
    mixed = depthwise(smoothed, v_half, 1).astype(jnp.bfloat16)
    weighted = cotangent * tissue.astype(jnp.bfloat16)[None]
    channels = features.shape[0]

    def to_blocks(source):
        return jnp.transpose(source.reshape(channels, N_BAND, -1), (1, 0, 2))

    def from_blocks(source):
        return jnp.transpose(source, (1, 0, 2)).reshape(features.shape)

    def one_block(couple):
        return pointwise(couple[0], couple[1], norm_gain, w_in, w_out)
    branch, grad_mixed = lax.map(one_block, (to_blocks(mixed), to_blocks(weighted)))
    branch = from_blocks(branch)
    grad_mixed = from_blocks(grad_mixed)
    block_out = (features.astype(jnp.float32) + branch.astype(jnp.float32)).astype(jnp.bfloat16)
    v_grad = tap_grad(smoothed, grad_mixed, 1, radius)
    grad_smooth = depthwise(grad_mixed, v_half[:, ::-1], 1).astype(jnp.bfloat16)
    h_grad = tap_grad(features, grad_smooth, 2, radius)
    squares = (lax.optimization_barrier(jnp.sum(h_grad * h_grad, axis=1)) + lax.optimization_barrier(jnp.sum(v_grad * v_grad, axis=1))) / (2 * K)
    inverse_rms = lax.rsqrt(squares + EPSILON)[:, None]
    h_new = h_kernel - STEP_SIZE * h_grad * inverse_rms
    v_new = v_kernel - STEP_SIZE * v_grad * inverse_rms
    h_swa = (AVERAGED * h_kernel_avg + h_new) / (AVERAGED + 1)
    v_swa = (AVERAGED * v_kernel_avg + v_new) / (AVERAGED + 1)
    return (block_out, h_new, v_new, h_swa, v_swa)
```

```python
import math

import jax
import jax.numpy as jnp
from jax import lax
from jax.experimental import pallas as pl
from jax.experimental.pallas import tpu as pltpu
from jax.sharding import PartitionSpec as P

AVERAGED = 4
EPSILON = 1e-06
STEP_SIZE = 0.1
ROOT_HALF = math.sqrt(0.5)
INV_ROOT_TWO_PI = 1.0 / math.sqrt(2.0 * math.pi)

MESH = pl.DeviceIdType.MESH
BF16 = jnp.bfloat16
F32 = jnp.float32

PLACES = 8
LEVELS = 16
COUNT_Y = 4
ROWS = 2 * PLACES
GROUPS = 6
GROUP = 16
LOCAL = GROUPS * GROUP
C = COUNT_Y * LOCAL
HID = 1536
K = 47
RADIUS = 23
W = 128
HALO = 24
TALL = ROWS + 2 * HALO
BLOCK = 256


def wait_bytes(view, sem):
    pltpu.make_async_copy(view, view, sem).wait()


def kernel(
    f_ref,
    w_ref,
    h_ref,
    v_ref,
    gain_ref,
    w_in_hbm,
    w_out_hbm,
    out_ref,
    up_ref,
    w_in,
    w_out,
    w_in_t,
    w_out_t,
    gain,
    taps,
    smoothed,
    tall_s,
    tall_f,
    wide_s,
    wide_f,
    v_taps,
    shifted,
    mixed,
    cell_grads,
    grad_act,
    cell_values,
    standard,
    inverse_rows,
    normed,
    activated,
    grad_pre,
    grad_cells,
    grad_rows,
    branch_cells,
    branch_rows,
    partial,
    partials,
    update,
    updates,
    load_sem,
    here_sem,
    rows_send,
    rows_recv,
    halo_send,
    halo_recv,
    cot_send,
    cot_recv,
    mix_send,
    mix_recv,
    back_send,
    back_recv,
    branch_send,
    branch_recv,
    sum_send,
    sum_recv,
    all_send,
    all_recv,
):
    band = lax.axis_index("band")
    y = lax.axis_index("chan")
    z = band // PLACES
    place = band % PLACES
    core = band % 2
    works = place < GROUPS
    idles = place >= GROUPS
    points = core == y // 2
    rests = core != y // 2
    my_row = 2 * place + y % 2
    level = z * PLACES

    def remote(src, dst, send, recv, to_band, to_y):
        return pltpu.make_async_remote_copy(
            src_ref=src,
            dst_ref=dst,
            send_sem=send,
            recv_sem=recv,
            device_id=(to_band, to_y),
            device_id_type=MESH,
        )

    def go(stays, src, dst, send, recv, here, to_band, to_y):
        @pl.when(stays)
        def _():
            pltpu.make_async_copy(src, dst, here).start()

        @pl.when(jnp.logical_not(stays))
        def _():
            remote(src, dst, send, recv, to_band, to_y).start()

    def loop(count):
        return lambda body: lax.fori_loop(0, count, lambda i, c: (body(i), c)[1], 0)

    barrier = pltpu.get_barrier_semaphore()

    @loop(PLACES * COUNT_Y)
    def _(i):
        to_place = i // COUNT_Y
        to_y = i % COUNT_Y

        @pl.when(jnp.logical_or(to_place != place, to_y != y))
        def _():
            pl.semaphore_signal(
                barrier, 1, device_id=(level + to_place, to_y), device_id_type=MESH
            )

    @loop(LEVELS)
    def _(i):
        @pl.when(jnp.logical_and(works, i != z))
        def _():
            pl.semaphore_signal(
                barrier, 1, device_id=(i * PLACES + place, y), device_id_type=MESH
            )

    load_in = pltpu.make_async_copy(w_in_hbm, w_in, load_sem.at[0])
    load_out = pltpu.make_async_copy(w_out_hbm, w_out, load_sem.at[1])
    load_in.start()
    load_out.start()

    taps[...] = jnp.zeros((2, W, W), F32)
    taps[0, 0:K, 0:LOCAL] = h_ref[...]
    taps[1, 0:K, 0:LOCAL] = v_ref[...]
    h_half = taps[0].T[0:LOCAL].astype(BF16).astype(F32)
    taps[1] = taps[1].T.astype(BF16).astype(F32)
    column = lax.broadcasted_iota(jnp.int32, (LOCAL, W), 1)
    sources = [f_ref[:, row].reshape(LOCAL, W).astype(F32) for row in range(2)]
    sums = [jnp.zeros((LOCAL, W), F32) for row in range(2)]
    for t in range(K):
        weight = jnp.broadcast_to(h_half[:, t : t + 1], (LOCAL, W))
        if t < RADIUS:
            weight = jnp.where(column >= RADIUS - t, weight, 0.0)
        if t > RADIUS:
            weight = jnp.where(column < W + RADIUS - t, weight, 0.0)
        for row in range(2):
            moved = sources[row]
            if t != RADIUS:
                moved = pltpu.roll(moved, (RADIUS - t) % W, 1)
            sums[row] = sums[row] + weight * moved
    for row in range(2):
        smoothed[:, row] = sums[row].astype(BF16).reshape(GROUPS, GROUP, W)

    @pl.when(works)
    def _():
        pl.semaphore_wait(barrier, PLACES * COUNT_Y - 1 + LEVELS - 1)

    @pl.when(idles)
    def _():
        pl.semaphore_wait(barrier, PLACES * COUNT_Y - 1)

    own_pair = pl.ds(HALO + 2 * place, 2)

    @loop(GROUPS)
    def _(g):
        go(
            g == place,
            smoothed.at[g],
            tall_s.at[own_pair],
            rows_send.at[0],
            rows_recv.at[0],
            here_sem.at[0],
            level + g,
            y,
        )

    for row in range(2):
        go(
            jnp.logical_and(points, y % 2 == row),
            w_ref.at[row],
            cell_grads.at[y],
            cot_send,
            cot_recv,
            here_sem.at[1],
            band,
            2 * core + row,
        )

    @loop(GROUPS)
    def _(g):
        go(
            g == place,
            f_ref.at[g],
            tall_f.at[own_pair],
            rows_send.at[1],
            rows_recv.at[1],
            here_sem.at[2],
            level + g,
            y,
        )

    moves = (
        (1, HALO, 8, ROWS),
        (-1, HALO, HALO + ROWS, ROWS),
        (2, HALO + 8, 0, 8),
        (-2, HALO, HALO + 2 * ROWS, 8),
    )

    def inside(step):
        return jnp.logical_and(z + step >= 0, z + step < LEVELS)

    def send_halo(tall, which):
        for m, (step, here, there, rows) in enumerate(moves):

            @pl.when(inside(step))
            def _(m=m, step=step, here=here, there=there, rows=rows):
                remote(
                    tall.at[pl.ds(here, rows)],
                    tall.at[pl.ds(there, rows)],
                    halo_send.at[which, m],
                    halo_recv.at[which, m],
                    (z + step) * PLACES + place,
                    y,
                ).start()

    def wait_halo(tall, which):
        for m, (step, here, there, rows) in enumerate(moves):

            @pl.when(inside(-step))
            def _(m=m, there=there, rows=rows):
                wait_bytes(tall.at[pl.ds(there, rows)], halo_recv.at[which, m])

            @pl.when(jnp.logical_not(inside(-step)))
            def _(there=there, rows=rows):
                tall[pl.ds(there, rows)] = jnp.zeros((rows, GROUP, W), BF16)

    @pl.when(works)
    def _():
        v_half = taps[1, pl.ds(pl.multiple_of(place * GROUP, GROUP), GROUP), :]
        for t in range(K):
            v_taps[t] = jnp.broadcast_to(v_half[:, t : t + 1], (GROUP, W))
        wait_bytes(tall_s.at[pl.ds(HALO, 14)], rows_recv.at[0])
        wait_bytes(tall_s.at[pl.ds(HALO, 2)], here_sem.at[0])
        send_halo(tall_s, 0)
        wait_bytes(tall_f.at[pl.ds(HALO, 14)], rows_recv.at[1])
        wait_bytes(tall_f.at[pl.ds(HALO, 2)], here_sem.at[2])
        send_halo(tall_f, 1)

    load_in.wait()
    load_out.wait()

    @pl.when(points)
    def _():
        gain[...] = jnp.broadcast_to(gain_ref[...], (W, C)).T

        @loop(HID // BLOCK)
        def _(i):
            at = pl.ds(pl.multiple_of(i * BLOCK, BLOCK), BLOCK)
            w_in_t[at, :] = w_in[:, at].T
            w_out_t[:, at] = w_out[at, :].T

        wait_bytes(cell_grads.at[pl.ds(0, 3)], cot_recv)
        wait_bytes(cell_grads.at[0], here_sem.at[1])
        upstream = cell_grads[...].reshape(C, W)

        @loop(HID // BLOCK)
        def _(i):
            at = pl.ds(pl.multiple_of(i * BLOCK, BLOCK), BLOCK)
            grad_act[at, :] = jnp.dot(w_out[at, :], upstream, preferred_element_type=F32)

    def row_convolution(wide):
        def tap(t, acc):
            return acc + v_taps[t][None] * wide[pl.ds(t + 1, ROWS)]

        return lax.fori_loop(0, K, tap, jnp.zeros((ROWS, GROUP, W), F32))

    @pl.when(works)
    def _():
        wait_halo(tall_s, 0)
        wide_s[...] = tall_s[...].astype(F32)
        mixed[...] = row_convolution(wide_s).astype(BF16)

        @loop(ROWS)
        def _(r):
            go(
                jnp.logical_and(points, r == my_row),
                mixed.at[r],
                cell_values.at[y * GROUPS + place],
                mix_send,
                mix_recv,
                here_sem.at[3],
                level + r // 2,
                r % COUNT_Y,
            )

    @pl.when(points)
    def _():
        @pl.when(works)
        def _():
            wait_bytes(cell_values.at[pl.ds(0, C // GROUP - 1)], mix_recv)
            wait_bytes(cell_values.at[0], here_sem.at[3])

        @pl.when(idles)
        def _():
            wait_bytes(cell_values, mix_recv)

        values = cell_values[...].reshape(C, W).astype(F32)
        centred = values - jnp.sum(values, axis=0, keepdims=True) * (1.0 / C)
        variance = jnp.sum(centred * centred, axis=0, keepdims=True) * (1.0 / C)
        inverse = lax.rsqrt(variance + EPSILON)
        scaled = centred * inverse
        standard[...] = scaled
        inverse_rows[...] = inverse
        normed[...] = (scaled * gain[...]).astype(BF16)

        @loop(HID // BLOCK)
        def _(i):
            at = pl.ds(pl.multiple_of(i * BLOCK, BLOCK), BLOCK)
            pre = jnp.dot(w_in_t[at, :], normed[...], preferred_element_type=F32)
            cumulative = 0.5 * (1.0 + lax.erf(pre * ROOT_HALF))
            activated[at, :] = (pre * cumulative).astype(BF16)
            density = jnp.exp(-0.5 * pre * pre) * INV_ROOT_TWO_PI
            grad_pre[at, :] = (grad_act[at, :] * (cumulative + pre * density)).astype(BF16)

        scaled = jnp.dot(w_in[...], grad_pre[...], preferred_element_type=F32) * gain[...]
        mean_scaled = jnp.sum(scaled, axis=0, keepdims=True) * (1.0 / C)
        mean_product = jnp.sum(scaled * standard[...], axis=0, keepdims=True) * (1.0 / C)
        back = (scaled - mean_scaled - standard[...] * mean_product) * inverse_rows[...]
        grad_cells[...] = back.astype(BF16).reshape(C // GROUP, GROUP, W)

        @loop(C // GROUP)
        def _(i):
            to_y = i // GROUPS
            to_place = i % GROUPS
            go(
                jnp.logical_and(to_y == y, to_place == place),
                grad_cells.at[i],
                grad_rows.at[my_row],
                back_send,
                back_recv,
                here_sem.at[4],
                level + to_place,
                to_y,
            )

        branch = jnp.dot(w_out_t[...], activated[...], preferred_element_type=F32)
        branch_cells[...] = branch.astype(BF16).reshape(COUNT_Y, LOCAL, W)

        @loop(COUNT_Y)
        def _(i):
            go(
                i == y,
                branch_cells.at[i],
                branch_rows.at[y % 2],
                branch_send,
                branch_recv,
                here_sem.at[5],
                band,
                i,
            )

    lane = lax.broadcasted_iota(jnp.int32, (GROUP, W), 1)

    @pl.when(works)
    def _():
        wait_halo(tall_f, 1)
        wide_f[...] = tall_f[...].astype(F32)
        rows_f = row_convolution(wide_f)
        column = lax.broadcasted_iota(jnp.int32, (ROWS * GROUP, W), 1)
        rows_f = rows_f.reshape(ROWS * GROUP, W)

        @loop(K)
        def _(t):
            moved = pltpu.roll(rows_f, lax.rem(W + RADIUS - t, W), 1)
            first = column + (t - RADIUS)
            moved = jnp.where(jnp.logical_and(first >= 0, first < W), moved, 0.0)
            shifted[t] = moved.reshape(ROWS, GROUP, W)

        @pl.when(points)
        def _():
            wait_bytes(grad_rows.at[pl.ds(0, ROWS - 1)], back_recv)
            wait_bytes(grad_rows.at[0], here_sem.at[4])

        @pl.when(rests)
        def _():
            wait_bytes(grad_rows, back_recv)

        grads = grad_rows[...].astype(F32)

        def tap(t, sums):
            v_sum = jnp.sum(grads * wide_s[pl.ds(t + 1, ROWS)], axis=0)
            h_sum = jnp.sum(grads * shifted[t], axis=0)
            sums = jnp.where(lane == t, jnp.sum(v_sum, axis=1, keepdims=True), sums)
            return jnp.where(lane == t + 64, jnp.sum(h_sum, axis=1, keepdims=True), sums)

        sums = lax.fori_loop(0, K, tap, jnp.zeros((GROUP, W), F32))
        partial[...] = sums
        partials[z] = sums

        @loop(LEVELS)
        def _(i):
            @pl.when(i != z)
            def _():
                remote(
                    partial,
                    partials.at[z],
                    sum_send,
                    sum_recv,
                    i * PLACES + place,
                    y,
                ).start()

    @pl.when(points)
    def _():
        wait_bytes(branch_rows.at[0], branch_recv)
        wait_bytes(branch_rows.at[0], here_sem.at[5])

    @pl.when(rests)
    def _():
        wait_bytes(branch_rows, branch_recv)

    for row in range(2):
        added = f_ref[:, row].reshape(LOCAL, W).astype(F32) + branch_rows[row].astype(F32)
        out_ref[row] = added.astype(BF16)

    @pl.when(works)
    def _():
        wait_bytes(partials.at[pl.ds(0, LEVELS - 1)], sum_recv)
        grads = partials[0]
        for i in range(1, LEVELS):
            grads = grads + partials[i]
        squares = jnp.sum(grads * grads, axis=1, keepdims=True) / (2 * K)
        steps = STEP_SIZE * grads * lax.rsqrt(squares + EPSILON)
        update[...] = steps
        updates[place] = steps

        @loop(PLACES)
        def _(i):
            @pl.when(i != place)
            def _():
                remote(
                    update,
                    updates.at[place],
                    all_send,
                    all_recv,
                    level + i,
                    y,
                ).start()

        wait_bytes(updates.at[pl.ds(0, GROUPS - 1)], all_recv)

    @pl.when(idles)
    def _():
        wait_bytes(updates.at[pl.ds(0, GROUPS)], all_recv)

    up_ref[...] = updates[...].reshape(W, W).T

    @pl.when(works)
    def _():
        for which, tall in enumerate((tall_s, tall_f)):
            wait_bytes(tall.at[pl.ds(0, 10)], rows_send.at[which])
            for m, (step, here, there, rows) in enumerate(moves):

                @pl.when(inside(step))
                def _(m=m, tall=tall, which=which, here=here, rows=rows):
                    wait_bytes(tall.at[pl.ds(here, rows)], halo_send.at[which, m])

        @pl.when(points)
        def _():
            wait_bytes(mixed.at[pl.ds(0, ROWS - 1)], mix_send)
            wait_bytes(grad_cells.at[pl.ds(0, C // GROUP - 1)], back_send)

        @pl.when(rests)
        def _():
            wait_bytes(mixed, mix_send)

        wait_bytes(partials.at[pl.ds(0, LEVELS - 1)], sum_send)
        wait_bytes(updates.at[pl.ds(0, PLACES - 1)], all_send)

    @pl.when(idles)
    def _():
        for which, tall in enumerate((tall_s, tall_f)):
            wait_bytes(tall.at[pl.ds(0, 12)], rows_send.at[which])

        @pl.when(points)
        def _():
            wait_bytes(grad_cells, back_send)

    @pl.when(points)
    def _():
        wait_bytes(cell_grads.at[0], cot_send)
        wait_bytes(branch_cells.at[pl.ds(0, COUNT_Y - 1)], branch_send)

    @pl.when(rests)
    def _():
        wait_bytes(cell_grads.at[pl.ds(0, 2)], cot_send)


def local(
    features,
    h_kernel,
    v_kernel,
    h_kernel_avg,
    v_kernel_avg,
    norm_gain,
    w_in,
    w_out,
    cotangent,
    tissue,
):
    grouped = jnp.transpose(features.reshape(GROUPS, GROUP, 2, W), (0, 2, 1, 3))
    weighted = jnp.transpose(cotangent * tissue.astype(BF16)[None], (1, 0, 2))
    vmem = pl.BlockSpec(memory_space=pltpu.VMEM)
    hbm = pl.BlockSpec(memory_space=pl.ANY)
    dma = pltpu.SemaphoreType.DMA
    out, step = pl.pallas_call(
        kernel,
        name="swa_step",
        out_shape=(
            jax.ShapeDtypeStruct((2, LOCAL, W), BF16),
            jax.ShapeDtypeStruct((W, W), F32),
        ),
        in_specs=[vmem] * 5 + [hbm] * 2,
        out_specs=(vmem, vmem),
        scratch_shapes=[
            pltpu.VMEM((C, HID), BF16),
            pltpu.VMEM((HID, C), BF16),
            pltpu.VMEM((HID, C), BF16),
            pltpu.VMEM((C, HID), BF16),
            pltpu.VMEM((C, W), F32),
            pltpu.VMEM((2, W, W), F32),
            pltpu.VMEM((GROUPS, 2, GROUP, W), BF16),
            pltpu.VMEM((TALL, GROUP, W), BF16),
            pltpu.VMEM((TALL, GROUP, W), BF16),
            pltpu.VMEM((TALL, GROUP, W), F32),
            pltpu.VMEM((TALL, GROUP, W), F32),
            pltpu.VMEM((K, GROUP, W), F32),
            pltpu.VMEM((K, ROWS, GROUP, W), F32),
            pltpu.VMEM((ROWS, GROUP, W), BF16),
            pltpu.VMEM((COUNT_Y, LOCAL, W), BF16),
            pltpu.VMEM((HID, W), F32),
            pltpu.VMEM((C // GROUP, GROUP, W), BF16),
            pltpu.VMEM((C, W), F32),
            pltpu.VMEM((1, W), F32),
            pltpu.VMEM((C, W), BF16),
            pltpu.VMEM((HID, W), BF16),
            pltpu.VMEM((HID, W), BF16),
            pltpu.VMEM((C // GROUP, GROUP, W), BF16),
            pltpu.VMEM((ROWS, GROUP, W), BF16),
            pltpu.VMEM((COUNT_Y, LOCAL, W), BF16),
            pltpu.VMEM((2, LOCAL, W), BF16),
            pltpu.VMEM((GROUP, W), F32),
            pltpu.VMEM((LEVELS, GROUP, W), F32),
            pltpu.VMEM((GROUP, W), F32),
            pltpu.VMEM((PLACES, GROUP, W), F32),
            dma((2,)),
            dma((6,)),
            dma((2,)),
            dma((2,)),
            dma((2, 4)),
            dma((2, 4)),
            dma,
            dma,
            dma,
            dma,
            dma,
            dma,
            dma,
            dma,
            dma,
            dma,
            dma,
            dma,
        ],
        compiler_params=pltpu.CompilerParams(collective_id=0, has_side_effects=True),
    )(
        grouped,
        weighted,
        h_kernel.T,
        v_kernel.T,
        norm_gain.reshape(1, C),
        w_in,
        w_out,
    )
    block_out = jnp.transpose(out, (1, 0, 2))
    v_new = v_kernel - step[0:K, 0:LOCAL].T
    h_new = h_kernel - step[64 : 64 + K, 0:LOCAL].T
    h_swa = (AVERAGED * h_kernel_avg + h_new) / (AVERAGED + 1)
    v_swa = (AVERAGED * v_kernel_avg + v_new) / (AVERAGED + 1)
    return (block_out, h_new, v_new, h_swa, v_swa)


def solution(mesh):
    return jax.shard_map(
        local,
        mesh=mesh,
        in_specs=(
            P("chan", "band", None),
            P("chan", None),
            P("chan", None),
            P("chan", None),
            P("chan", None),
            P(),
            P(),
            P(),
            P("chan", "band", None),
            P("band", None),
        ),
        out_specs=(
            P("chan", "band", None),
            P("chan", None),
            P("chan", None),
            P("chan", None),
            P("chan", None),
        ),
        check_vma=False,
    )
```

```python
import math

import jax
import jax.numpy as jnp
from jax import lax
from jax.experimental import pallas as pl
from jax.experimental.pallas import tpu as pltpu
from jax.sharding import PartitionSpec as P

AVERAGED = 4
EPSILON = 1e-06
STEP_SIZE = 0.1
ROOT_HALF = math.sqrt(0.5)
INV_ROOT_TWO_PI = 1.0 / math.sqrt(2.0 * math.pi)

MESH = pl.DeviceIdType.MESH
BF16 = jnp.bfloat16
F32 = jnp.float32

PLACES = 8
LEVELS = 16
COUNT_Y = 4
ROWS = 2 * PLACES
GROUPS = 6
GROUP = 16
LOCAL = GROUPS * GROUP
C = COUNT_Y * LOCAL
HID = 1536
K = 47
RADIUS = 23
W = 128
HALO = 24
TALL = ROWS + 2 * HALO
BLOCK = 256


def wait_bytes(view, sem):
    pltpu.make_async_copy(view, view, sem).wait()


def kernel(
    f_hbm,
    cot_hbm,
    tissue_ref,
    h_ref,
    v_ref,
    gain_ref,
    w_in_hbm,
    w_out_hbm,
    out_ref,
    up_ref,
    f_pairs,
    cot_pairs,
    f_rows,
    w_rows,
    w_in,
    w_out,
    w_in_t,
    w_out_t,
    gain,
    taps,
    smoothed,
    tall_s,
    tall_f,
    wide_s,
    wide_f,
    v_taps,
    shifted,
    mixed,
    cell_grads,
    grad_act,
    cell_values,
    standard,
    inverse_rows,
    normed,
    activated,
    grad_pre,
    grad_cells,
    grad_rows,
    branch_cells,
    branch_rows,
    partial,
    partials,
    update,
    updates,
    far_sem,
    load_sem,
    here_sem,
    rows_send,
    rows_recv,
    halo_send,
    halo_recv,
    cot_send,
    cot_recv,
    mix_send,
    mix_recv,
    back_send,
    back_recv,
    branch_send,
    branch_recv,
    sum_send,
    sum_recv,
    all_send,
    all_recv,
):
    band = lax.axis_index("band")
    y = lax.axis_index("chan")
    z = band // PLACES
    place = band % PLACES
    core = band % 2
    works = place < GROUPS
    idles = place >= GROUPS
    points = core == y // 2
    rests = core != y // 2
    my_row = 2 * place + y % 2
    level = z * PLACES

    def remote(src, dst, send, recv, to_band, to_y):
        return pltpu.make_async_remote_copy(
            src_ref=src,
            dst_ref=dst,
            send_sem=send,
            recv_sem=recv,
            device_id=(to_band, to_y),
            device_id_type=MESH,
        )

    def go(stays, src, dst, send, recv, here, to_band, to_y):
        @pl.when(stays)
        def _():
            pltpu.make_async_copy(src, dst, here).start()

        @pl.when(jnp.logical_not(stays))
        def _():
            remote(src, dst, send, recv, to_band, to_y).start()

    def loop(count):
        return lambda body: lax.fori_loop(0, count, lambda i, c: (body(i), c)[1], 0)

    barrier = pltpu.get_barrier_semaphore()

    @loop(PLACES * COUNT_Y)
    def _(i):
        to_place = i // COUNT_Y
        to_y = i % COUNT_Y

        @pl.when(jnp.logical_or(to_place != place, to_y != y))
        def _():
            pl.semaphore_signal(
                barrier, 1, device_id=(level + to_place, to_y), device_id_type=MESH
            )

    def tell(sem, step):
        there = lax.rem(z + step + LEVELS, LEVELS)
        pl.semaphore_signal(
            sem, 1, device_id=(there * PLACES + place, y), device_id_type=MESH
        )

    @pl.when(works)
    def _():
        for step in (1, -1, 2, -2):
            tell(barrier, step)

    load_in = pltpu.make_async_copy(w_in_hbm, w_in, load_sem.at[0])
    load_out = pltpu.make_async_copy(w_out_hbm, w_out, load_sem.at[1])
    load_f = pltpu.make_async_copy(f_hbm, f_pairs, load_sem.at[2])
    load_cot = pltpu.make_async_copy(cot_hbm, cot_pairs, load_sem.at[3])
    for load in (load_f, load_cot, load_in, load_out):
        load.start()

    taps[...] = jnp.zeros((2, W, W), F32)
    taps[0, 0:K, 0:LOCAL] = h_ref[...]
    taps[1, 0:K, 0:LOCAL] = v_ref[...]
    h_half = taps[0].T[0:LOCAL].astype(BF16).astype(F32)
    taps[1] = taps[1].T.astype(BF16).astype(F32)
    column = lax.broadcasted_iota(jnp.int32, (LOCAL, W), 1)
    load_f.wait()
    sources = [f_pairs[:, row, :].astype(F32) for row in range(2)]
    for row in range(2):
        f_rows[:, row] = sources[row].astype(BF16).reshape(GROUPS, GROUP, W)
    sums = [jnp.zeros((LOCAL, W), F32) for row in range(2)]
    for t in range(K):
        weight = jnp.broadcast_to(h_half[:, t : t + 1], (LOCAL, W))
        if t < RADIUS:
            weight = jnp.where(column >= RADIUS - t, weight, 0.0)
        if t > RADIUS:
            weight = jnp.where(column < W + RADIUS - t, weight, 0.0)
        for row in range(2):
            moved = sources[row]
            if t != RADIUS:
                moved = pltpu.roll(moved, (RADIUS - t) % W, 1)
            sums[row] = sums[row] + weight * moved
    for row in range(2):
        smoothed[:, row] = sums[row].astype(BF16).reshape(GROUPS, GROUP, W)
    load_cot.wait()
    for row in range(2):
        mask = tissue_ref[row : row + 1, :].astype(F32)
        w_rows[row] = (cot_pairs[:, row, :].astype(F32) * mask).astype(BF16)

    @pl.when(works)
    def _():
        pl.semaphore_wait(barrier, PLACES * COUNT_Y - 1 + 4)
        tell(far_sem.at[0], 2)
        tell(far_sem.at[0], -2)

    @pl.when(idles)
    def _():
        pl.semaphore_wait(barrier, PLACES * COUNT_Y - 1)

    own_pair = pl.ds(HALO + 2 * place, 2)

    @loop(GROUPS)
    def _(g):
        go(
            g == place,
            smoothed.at[g],
            tall_s.at[own_pair],
            rows_send.at[0],
            rows_recv.at[0],
            here_sem.at[0],
            level + g,
            y,
        )

    for row in range(2):
        go(
            jnp.logical_and(points, y % 2 == row),
            w_rows.at[row],
            cell_grads.at[y],
            cot_send,
            cot_recv,
            here_sem.at[1],
            band,
            2 * core + row,
        )

    @loop(GROUPS)
    def _(g):
        go(
            g == place,
            f_rows.at[g],
            tall_f.at[own_pair],
            rows_send.at[1],
            rows_recv.at[1],
            here_sem.at[2],
            level + g,
            y,
        )

    moves = (
        (1, HALO, 8, ROWS),
        (-1, HALO, HALO + ROWS, ROWS),
        (2, HALO + 8, 0, 8),
        (-2, HALO, HALO + 2 * ROWS, 8),
    )

    def inside(step):
        return jnp.logical_and(z + step >= 0, z + step < LEVELS)

    def send_halo(tall, which):
        for m, (step, here, there, rows) in enumerate(moves):

            @pl.when(inside(step))
            def _(m=m, step=step, here=here, there=there, rows=rows):
                remote(
                    tall.at[pl.ds(here, rows)],
                    tall.at[pl.ds(there, rows)],
                    halo_send.at[which, m],
                    halo_recv.at[which, m],
                    (z + step) * PLACES + place,
                    y,
                ).start()

    def wait_halo(tall, which):
        for m, (step, here, there, rows) in enumerate(moves):

            @pl.when(inside(-step))
            def _(m=m, there=there, rows=rows):
                wait_bytes(tall.at[pl.ds(there, rows)], halo_recv.at[which, m])

            @pl.when(jnp.logical_not(inside(-step)))
            def _(there=there, rows=rows):
                tall[pl.ds(there, rows)] = jnp.zeros((rows, GROUP, W), BF16)

    @pl.when(works)
    def _():
        v_half = taps[1, pl.ds(pl.multiple_of(place * GROUP, GROUP), GROUP), :]
        for t in range(K):
            v_taps[t] = jnp.broadcast_to(v_half[:, t : t + 1], (GROUP, W))
        wait_bytes(tall_s.at[pl.ds(HALO, 14)], rows_recv.at[0])
        wait_bytes(tall_s.at[pl.ds(HALO, 2)], here_sem.at[0])
        send_halo(tall_s, 0)
        wait_bytes(tall_f.at[pl.ds(HALO, 14)], rows_recv.at[1])
        wait_bytes(tall_f.at[pl.ds(HALO, 2)], here_sem.at[2])
        send_halo(tall_f, 1)

    load_in.wait()
    load_out.wait()

    @pl.when(points)
    def _():
        for i in range(C // W):
            gain[i * W : (i + 1) * W] = jnp.broadcast_to(gain_ref[i : i + 1, :], (W, W)).T

        @loop(HID // BLOCK)
        def _(i):
            at = pl.ds(pl.multiple_of(i * BLOCK, BLOCK), BLOCK)
            w_in_t[at, :] = w_in[:, at].T
            w_out_t[:, at] = w_out[at, :].T

        wait_bytes(cell_grads.at[pl.ds(0, 3)], cot_recv)
        wait_bytes(cell_grads.at[0], here_sem.at[1])
        upstream = cell_grads[...].reshape(C, W)

        @loop(HID // BLOCK)
        def _(i):
            at = pl.ds(pl.multiple_of(i * BLOCK, BLOCK), BLOCK)
            grad_act[at, :] = jnp.dot(w_out[at, :], upstream, preferred_element_type=F32)


    def row_convolution(wide):
        def tap(t, acc):
            return acc + v_taps[t][None] * wide[pl.ds(t + 1, ROWS)]

        acc = jnp.zeros((ROWS, GROUP, W), F32)
        for t in range(K):
            acc = tap(t, acc)
        return acc

    @pl.when(works)
    def _():
        wait_halo(tall_s, 0)
        wide_s[...] = tall_s[...].astype(F32)
        mixed[...] = row_convolution(wide_s).astype(BF16)

        @loop(ROWS)
        def _(r):
            go(
                jnp.logical_and(points, r == my_row),
                mixed.at[r],
                cell_values.at[y * GROUPS + place],
                mix_send,
                mix_recv,
                here_sem.at[3],
                level + r // 2,
                r % COUNT_Y,
            )


    @pl.when(points)
    def _():
        @pl.when(works)
        def _():
            wait_bytes(cell_values.at[pl.ds(0, C // GROUP - 1)], mix_recv)
            wait_bytes(cell_values.at[0], here_sem.at[3])

        @pl.when(idles)
        def _():
            wait_bytes(cell_values, mix_recv)

        values = cell_values[...].reshape(C, W).astype(F32)
        centred = values - jnp.sum(values, axis=0, keepdims=True) * (1.0 / C)
        variance = jnp.sum(centred * centred, axis=0, keepdims=True) * (1.0 / C)
        inverse = lax.rsqrt(variance + EPSILON)
        scaled = centred * inverse
        standard[...] = scaled
        inverse_rows[...] = inverse
        normed[...] = (scaled * gain[...]).astype(BF16)

        @loop(HID // BLOCK)
        def _(i):
            at = pl.ds(pl.multiple_of(i * BLOCK, BLOCK), BLOCK)
            pre = jnp.dot(w_in_t[at, :], normed[...], preferred_element_type=F32)
            cumulative = 0.5 * (1.0 + lax.erf(pre * ROOT_HALF))
            activated[at, :] = (pre * cumulative).astype(BF16)
            density = jnp.exp(-0.5 * pre * pre) * INV_ROOT_TWO_PI
            grad_pre[at, :] = (grad_act[at, :] * (cumulative + pre * density)).astype(BF16)

        scaled = jnp.dot(w_in[...], grad_pre[...], preferred_element_type=F32) * gain[...]
        mean_scaled = jnp.sum(scaled, axis=0, keepdims=True) * (1.0 / C)
        mean_product = jnp.sum(scaled * standard[...], axis=0, keepdims=True) * (1.0 / C)
        back = (scaled - mean_scaled - standard[...] * mean_product) * inverse_rows[...]
        grad_cells[...] = back.astype(BF16).reshape(C // GROUP, GROUP, W)

        @loop(C // GROUP)
        def _(i):
            to_y = i // GROUPS
            to_place = i % GROUPS
            go(
                jnp.logical_and(to_y == y, to_place == place),
                grad_cells.at[i],
                grad_rows.at[my_row],
                back_send,
                back_recv,
                here_sem.at[4],
                level + to_place,
                to_y,
            )

        branch = jnp.dot(w_out_t[...], activated[...], preferred_element_type=F32)
        branch_cells[...] = branch.astype(BF16).reshape(COUNT_Y, LOCAL, W)

        @loop(COUNT_Y)
        def _(i):
            go(
                i == y,
                branch_cells.at[i],
                branch_rows.at[y % 2],
                branch_send,
                branch_recv,
                here_sem.at[5],
                band,
                i,
            )


    lane = lax.broadcasted_iota(jnp.int32, (GROUP, W), 1)

    @pl.when(works)
    def _():
        pl.semaphore_wait(far_sem.at[0], 2)
        tell(far_sem.at[1], 4)
        tell(far_sem.at[1], -4)
        wait_halo(tall_f, 1)
        wide_f[...] = tall_f[...].astype(F32)
        rows_f = row_convolution(wide_f)
        column = lax.broadcasted_iota(jnp.int32, (ROWS * GROUP, W), 1)
        rows_f = rows_f.reshape(ROWS * GROUP, W)

        @loop(K)
        def _(t):
            moved = pltpu.roll(rows_f, lax.rem(W + RADIUS - t, W), 1)
            first = column + (t - RADIUS)
            moved = jnp.where(jnp.logical_and(first >= 0, first < W), moved, 0.0)
            shifted[t] = moved.reshape(ROWS, GROUP, W)

        @pl.when(points)
        def _():
            wait_bytes(grad_rows.at[pl.ds(0, ROWS - 1)], back_recv)
            wait_bytes(grad_rows.at[0], here_sem.at[4])

        @pl.when(rests)
        def _():
            wait_bytes(grad_rows, back_recv)

        grads = grad_rows[...].astype(F32)

        def tap(t, sums):
            v_sum = jnp.sum(grads * wide_s[pl.ds(t + 1, ROWS)], axis=0)
            h_sum = jnp.sum(grads * shifted[t], axis=0)
            sums = jnp.where(lane == t, jnp.sum(v_sum, axis=1, keepdims=True), sums)
            return jnp.where(lane == t + 64, jnp.sum(h_sum, axis=1, keepdims=True), sums)

        sums = jnp.zeros((GROUP, W), F32)
        for t in range(K):
            sums = tap(t, sums)
        partial[...] = sums.astype(BF16)
        partials[z] = sums.astype(BF16)
        pl.semaphore_wait(far_sem.at[1], 2)

        @loop(LEVELS)
        def _(i):
            @pl.when(i != z)
            def _():
                remote(
                    partial,
                    partials.at[z],
                    sum_send,
                    sum_recv,
                    i * PLACES + place,
                    y,
                ).start()


    @pl.when(points)
    def _():
        wait_bytes(branch_rows.at[0], branch_recv)
        wait_bytes(branch_rows.at[0], here_sem.at[5])

    @pl.when(rests)
    def _():
        wait_bytes(branch_rows, branch_recv)

    for row in range(2):
        added = f_rows[:, row].reshape(LOCAL, W).astype(F32) + branch_rows[row].astype(F32)
        out_ref[row] = added.astype(BF16)

    @pl.when(works)
    def _():
        wait_bytes(partials.at[pl.ds(0, LEVELS - 1)], sum_recv)
        grads = jnp.sum(partials[...].astype(F32), axis=0)
        squares = jnp.sum(grads * grads, axis=1, keepdims=True) / (2 * K)
        steps = STEP_SIZE * grads * lax.rsqrt(squares + EPSILON)
        update[...] = steps
        updates[place] = steps

        @loop(PLACES)
        def _(i):
            @pl.when(i != place)
            def _():
                remote(
                    update,
                    updates.at[place],
                    all_send,
                    all_recv,
                    level + i,
                    y,
                ).start()

        wait_bytes(updates.at[pl.ds(0, GROUPS - 1)], all_recv)

    @pl.when(idles)
    def _():
        wait_bytes(updates.at[pl.ds(0, GROUPS)], all_recv)

    up_ref[...] = updates[...].reshape(W, W).T

    @pl.when(works)
    def _():
        for which, tall in enumerate((tall_s, tall_f)):
            wait_bytes(tall.at[pl.ds(0, 10)], rows_send.at[which])
            for m, (step, here, there, rows) in enumerate(moves):

                @pl.when(inside(step))
                def _(m=m, tall=tall, which=which, here=here, rows=rows):
                    wait_bytes(tall.at[pl.ds(here, rows)], halo_send.at[which, m])

        @pl.when(points)
        def _():
            wait_bytes(mixed.at[pl.ds(0, ROWS - 1)], mix_send)
            wait_bytes(grad_cells.at[pl.ds(0, C // GROUP - 1)], back_send)

        @pl.when(rests)
        def _():
            wait_bytes(mixed, mix_send)

        wait_bytes(partials.at[pl.ds(0, LEVELS - 1)], sum_send)
        wait_bytes(updates.at[pl.ds(0, PLACES - 1)], all_send)

    @pl.when(idles)
    def _():
        for which, tall in enumerate((tall_s, tall_f)):
            wait_bytes(tall.at[pl.ds(0, 12)], rows_send.at[which])

        @pl.when(points)
        def _():
            wait_bytes(grad_cells, back_send)

    @pl.when(points)
    def _():
        wait_bytes(cell_grads.at[0], cot_send)
        wait_bytes(branch_cells.at[pl.ds(0, COUNT_Y - 1)], branch_send)

    @pl.when(rests)
    def _():
        wait_bytes(cell_grads.at[pl.ds(0, 2)], cot_send)


def finish(
    out_rows, step_ref, h_ref, v_ref, h_avg, v_avg, out_ref, h_new, v_new, h_swa, v_swa
):
    for row in range(2):
        out_ref[:, row, :] = out_rows[row]
    new = h_ref[...] - step_ref[64 : 64 + K, 0:LOCAL]
    h_new[...] = new
    h_swa[...] = (AVERAGED * h_avg[...] + new) / (AVERAGED + 1)
    new = v_ref[...] - step_ref[0:K, 0:LOCAL]
    v_new[...] = new
    v_swa[...] = (AVERAGED * v_avg[...] + new) / (AVERAGED + 1)


def local(
    features,
    h_kernel,
    v_kernel,
    h_kernel_avg,
    v_kernel_avg,
    norm_gain,
    w_in,
    w_out,
    cotangent,
    tissue,
):
    vmem = pl.BlockSpec(memory_space=pltpu.VMEM)
    hbm = pl.BlockSpec(memory_space=pl.ANY)
    dma = pltpu.SemaphoreType.DMA
    out, step = pl.pallas_call(
        kernel,
        name="swa_step",
        out_shape=(
            jax.ShapeDtypeStruct((2, LOCAL, W), BF16),
            jax.ShapeDtypeStruct((W, W), F32),
        ),
        in_specs=[hbm] * 2 + [vmem] * 4 + [hbm] * 2,
        out_specs=(vmem, vmem),
        scratch_shapes=[
            pltpu.VMEM((LOCAL, 2, W), BF16),
            pltpu.VMEM((LOCAL, 2, W), BF16),
            pltpu.VMEM((GROUPS, 2, GROUP, W), BF16),
            pltpu.VMEM((2, LOCAL, W), BF16),
            pltpu.VMEM((C, HID), BF16),
            pltpu.VMEM((HID, C), BF16),
            pltpu.VMEM((HID, C), BF16),
            pltpu.VMEM((C, HID), BF16),
            pltpu.VMEM((C, W), F32),
            pltpu.VMEM((2, W, W), F32),
            pltpu.VMEM((GROUPS, 2, GROUP, W), BF16),
            pltpu.VMEM((TALL, GROUP, W), BF16),
            pltpu.VMEM((TALL, GROUP, W), BF16),
            pltpu.VMEM((TALL, GROUP, W), F32),
            pltpu.VMEM((TALL, GROUP, W), F32),
            pltpu.VMEM((K, GROUP, W), F32),
            pltpu.VMEM((K, ROWS, GROUP, W), F32),
            pltpu.VMEM((ROWS, GROUP, W), BF16),
            pltpu.VMEM((COUNT_Y, LOCAL, W), BF16),
            pltpu.VMEM((HID, W), F32),
            pltpu.VMEM((C // GROUP, GROUP, W), BF16),
            pltpu.VMEM((C, W), F32),
            pltpu.VMEM((1, W), F32),
            pltpu.VMEM((C, W), BF16),
            pltpu.VMEM((HID, W), BF16),
            pltpu.VMEM((HID, W), BF16),
            pltpu.VMEM((C // GROUP, GROUP, W), BF16),
            pltpu.VMEM((ROWS, GROUP, W), BF16),
            pltpu.VMEM((COUNT_Y, LOCAL, W), BF16),
            pltpu.VMEM((2, LOCAL, W), BF16),
            pltpu.VMEM((GROUP, W), BF16),
            pltpu.VMEM((LEVELS, GROUP, W), BF16),
            pltpu.VMEM((GROUP, W), F32),
            pltpu.VMEM((PLACES, GROUP, W), F32),
            pltpu.SemaphoreType.REGULAR((2,)),
            dma((4,)),
            dma((6,)),
            dma((2,)),
            dma((2,)),
            dma((2, 4)),
            dma((2, 4)),
            dma,
            dma,
            dma,
            dma,
            dma,
            dma,
            dma,
            dma,
            dma,
            dma,
            dma,
            dma,
        ],
        compiler_params=pltpu.CompilerParams(collective_id=0, has_side_effects=True),
    )(
        features,
        cotangent,
        tissue,
        h_kernel.T,
        v_kernel.T,
        norm_gain.reshape(C // W, W),
        w_in,
        w_out,
    )
    taps = jax.ShapeDtypeStruct((K, LOCAL), F32)
    block_out, h_new, v_new, h_swa, v_swa = pl.pallas_call(
        finish,
        name="finish",
        out_shape=(jax.ShapeDtypeStruct((LOCAL, 2, W), BF16), taps, taps, taps, taps),
        in_specs=[vmem] * 6,
        out_specs=(vmem,) * 5,
    )(out, step, h_kernel.T, v_kernel.T, h_kernel_avg.T, v_kernel_avg.T)
    return (block_out, h_new.T, v_new.T, h_swa.T, v_swa.T)


def solution(mesh):
    return jax.shard_map(
        local,
        mesh=mesh,
        in_specs=(
            P("chan", "band", None),
            P("chan", None),
            P("chan", None),
            P("chan", None),
            P("chan", None),
            P(),
            P(),
            P(),
            P("chan", "band", None),
            P("band", None),
        ),
        out_specs=(
            P("chan", "band", None),
            P("chan", None),
            P("chan", None),
            P("chan", None),
            P("chan", None),
        ),
        check_vma=False,
    )
```

```python
import math

import jax
import jax.numpy as jnp
from jax import lax
from jax.experimental import pallas as pl
from jax.experimental.pallas import tpu as pltpu
from jax.sharding import PartitionSpec as P

AVERAGED = 4
EPSILON = 1e-06
STEP_SIZE = 0.1
ROOT_HALF = math.sqrt(0.5)
INV_ROOT_TWO_PI = 1.0 / math.sqrt(2.0 * math.pi)

MESH = pl.DeviceIdType.MESH
BF16 = jnp.bfloat16
F32 = jnp.float32

PLACES = 8
LEVELS = 16
COUNT_Y = 4
ROWS = 2 * PLACES
GROUPS = 6
GROUP = 16
LOCAL = GROUPS * GROUP
C = COUNT_Y * LOCAL
HID = 1536
K = 47
RADIUS = 23
W = 128
HALO = 24
TALL = ROWS + 2 * HALO
BLOCK = 256


def wait_bytes(view, sem):
    pltpu.make_async_copy(view, view, sem).wait()


def kernel(
    f_hbm,
    cot_hbm,
    tissue_hbm,
    h_hbm,
    v_hbm,
    gain_hbm,
    w_in_hbm,
    w_out_hbm,
    out_hbm,
    updates,
    tissue_ref,
    h_ref,
    v_ref,
    gain_ref,
    out_rows,
    f_pairs,
    cot_pairs,
    f_rows,
    w_rows,
    w_in,
    w_out,
    w_in_t,
    w_out_t,
    gain,
    taps,
    smoothed,
    tall_s,
    tall_f,
    wide_s,
    wide_f,
    v_taps,
    shifted,
    mixed,
    cell_grads,
    grad_act,
    cell_values,
    standard,
    inverse_rows,
    normed,
    activated,
    grad_pre,
    grad_cells,
    grad_rows,
    branch_cells,
    branch_rows,
    partial,
    partials,
    update,
    far_sem,
    load_sem,
    here_sem,
    rows_send,
    rows_recv,
    halo_send,
    halo_recv,
    cot_send,
    cot_recv,
    mix_send,
    mix_recv,
    back_send,
    back_recv,
    branch_send,
    branch_recv,
    sum_send,
    sum_recv,
    all_send,
    all_recv,
):
    band = lax.axis_index("band")
    y = lax.axis_index("chan")
    z = band // PLACES
    place = band % PLACES
    core = band % 2
    works = place < GROUPS
    idles = place >= GROUPS
    points = core == y // 2
    rests = core != y // 2
    my_row = 2 * place + y % 2
    level = z * PLACES

    def remote(src, dst, send, recv, to_band, to_y):
        return pltpu.make_async_remote_copy(
            src_ref=src,
            dst_ref=dst,
            send_sem=send,
            recv_sem=recv,
            device_id=(to_band, to_y),
            device_id_type=MESH,
        )

    def go(stays, src, dst, send, recv, here, to_band, to_y):
        @pl.when(stays)
        def _():
            pltpu.make_async_copy(src, dst, here).start()

        @pl.when(jnp.logical_not(stays))
        def _():
            remote(src, dst, send, recv, to_band, to_y).start()

    def loop(count):
        return lambda body: [body(i) for i in range(count)]

    barrier = pltpu.get_barrier_semaphore()

    for step in range(1, PLACES):
        line = level + lax.rem(place + step, PLACES)
        pl.semaphore_signal(barrier, 1, device_id=(line, y), device_id_type=MESH)
    others = [lax.rem(y + step, COUNT_Y) for step in range(1, COUNT_Y)]
    for to_y in others:
        pl.semaphore_signal(barrier, 1, device_id=(band, to_y), device_id_type=MESH)

    def tell(sem, step):
        there = lax.rem(z + step + LEVELS, LEVELS)
        pl.semaphore_signal(
            sem, 1, device_id=(there * PLACES + place, y), device_id_type=MESH
        )

    @pl.when(works)
    def _():
        for step in (1, -1, 2, -2):
            tell(barrier, step)

    load_in = pltpu.make_async_copy(w_in_hbm, w_in, load_sem.at[0])
    load_out = pltpu.make_async_copy(w_out_hbm, w_out, load_sem.at[1])
    load_f = pltpu.make_async_copy(f_hbm, f_pairs, load_sem.at[2])
    load_cot = pltpu.make_async_copy(cot_hbm, cot_pairs, load_sem.at[3])
    small = [
        pltpu.make_async_copy(src, dst, load_sem.at[4 + i])
        for i, (src, dst) in enumerate(
            ((h_hbm, h_ref), (v_hbm, v_ref), (tissue_hbm, tissue_ref), (gain_hbm, gain_ref))
        )
    ]
    for load in (load_f, *small, load_cot, load_in, load_out):
        load.start()

    for load in small:
        load.wait()
    taps[...] = jnp.zeros((2, W, W), F32)
    taps[0, 0:K, 0:LOCAL] = h_ref[...]
    taps[1, 0:K, 0:LOCAL] = v_ref[...]
    h_half = taps[0].T[0:LOCAL].astype(BF16).astype(F32)
    taps[1] = taps[1].T.astype(BF16).astype(F32)
    column = lax.broadcasted_iota(jnp.int32, (LOCAL, W), 1)
    load_f.wait()
    sources = [f_pairs[:, row, :].astype(F32) for row in range(2)]
    for row in range(2):
        f_rows[:, row] = sources[row].astype(BF16).reshape(GROUPS, GROUP, W)
    sums = [jnp.zeros((LOCAL, W), F32) for row in range(2)]
    for t in range(K):
        weight = jnp.broadcast_to(h_half[:, t : t + 1], (LOCAL, W))
        if t < RADIUS:
            weight = jnp.where(column >= RADIUS - t, weight, 0.0)
        if t > RADIUS:
            weight = jnp.where(column < W + RADIUS - t, weight, 0.0)
        for row in range(2):
            moved = sources[row]
            if t != RADIUS:
                moved = pltpu.roll(moved, (RADIUS - t) % W, 1)
            sums[row] = sums[row] + weight * moved
    for row in range(2):
        smoothed[:, row] = sums[row].astype(BF16).reshape(GROUPS, GROUP, W)
    load_cot.wait()
    for row in range(2):
        mask = tissue_ref[row : row + 1, :].astype(F32)
        w_rows[row] = (cot_pairs[:, row, :].astype(F32) * mask).astype(BF16)

    @pl.when(works)
    def _():
        pl.semaphore_wait(barrier, PLACES - 1 + COUNT_Y - 1 + 4)
        tell(far_sem.at[0], 2)
        tell(far_sem.at[0], -2)

    @pl.when(idles)
    def _():
        pl.semaphore_wait(barrier, PLACES - 1 + COUNT_Y - 1)

    for to_y in others:
        pl.semaphore_signal(far_sem.at[2], 1, device_id=(band, to_y), device_id_type=MESH)

    own_pair = pl.ds(HALO + 2 * place, 2)

    @loop(GROUPS)
    def _(g):
        go(
            g == place,
            smoothed.at[g],
            tall_s.at[own_pair],
            rows_send.at[0],
            rows_recv.at[place],
            here_sem.at[0],
            level + g,
            y,
        )

    for row in range(2):
        go(
            jnp.logical_and(points, y % 2 == row),
            w_rows.at[row],
            cell_grads.at[y],
            cot_send,
            cot_recv,
            here_sem.at[1],
            band,
            2 * core + row,
        )

    @loop(GROUPS)
    def _(g):
        go(
            g == place,
            f_rows.at[g],
            tall_f.at[own_pair],
            rows_send.at[1],
            rows_recv.at[PLACES],
            here_sem.at[2],
            level + g,
            y,
        )

    moves = (
        (1, HALO, 8, ROWS),
        (-1, HALO, HALO + ROWS, ROWS),
        (2, HALO + 8, 0, 8),
        (-2, HALO, HALO + 2 * ROWS, 8),
    )

    def inside(step):
        return jnp.logical_and(z + step >= 0, z + step < LEVELS)

    def send_halo(tall, which):
        for m, (step, here, there, rows) in enumerate(moves):

            @pl.when(inside(step))
            def _(m=m, step=step, here=here, there=there, rows=rows):
                remote(
                    tall.at[pl.ds(here, rows)],
                    tall.at[pl.ds(there, rows)],
                    halo_send.at[which, m],
                    halo_recv.at[which, m],
                    (z + step) * PLACES + place,
                    y,
                ).start()

    def wait_halo(tall, which):
        for m, (step, here, there, rows) in enumerate(moves):

            @pl.when(inside(-step))
            def _(m=m, there=there, rows=rows):
                wait_bytes(tall.at[pl.ds(there, rows)], halo_recv.at[which, m])

            @pl.when(jnp.logical_not(inside(-step)))
            def _(there=there, rows=rows):
                tall[pl.ds(there, rows)] = jnp.zeros((rows, GROUP, W), BF16)

    @pl.when(works)
    def _():
        v_half = taps[1, pl.ds(pl.multiple_of(place * GROUP, GROUP), GROUP), :]
        for t in range(K):
            v_taps[t] = jnp.broadcast_to(v_half[:, t : t + 1], (GROUP, W))
        for hop, flip in ((0, 0), (0, 1), (1, 0), (1, 1), (3, 0), (3, 1), (2, 0), (2, 1)):
            source = lax.rem(place + 2 * hop, PLACES)
            if flip:
                source = source + 1 - 2 * core
            pair = tall_s.at[pl.ds(HALO + 2 * source, 2)]
            if hop == 0 and flip == 0:
                wait_bytes(pair, here_sem.at[0])
            else:
                wait_bytes(pair, rows_recv.at[source])
            upper = source >= PLACES // 2
            far = jnp.where(upper, 2, -2)
            far_row = jnp.where(upper, 2 * source - 8, HALO + 2 * ROWS + 2 * source)
            far_m = jnp.where(upper, 2, 3)
            for m, step, row in (
                (far_m, far, far_row),
                (0, 1, 8 + 2 * source),
                (1, -1, HALO + ROWS + 2 * source),
            ):

                @pl.when(inside(step))
                def _(m=m, step=step, row=row, pair=pair):
                    remote(
                        pair,
                        tall_s.at[pl.ds(row, 2)],
                        halo_send.at[0, m],
                        halo_recv.at[0, m],
                        (z + step) * PLACES + place,
                        y,
                    ).start()


    load_in.wait()
    load_out.wait()
    pl.semaphore_wait(far_sem.at[2], COUNT_Y - 1)

    @pl.when(points)
    def _():
        for i in range(C // W):
            gain[i * W : (i + 1) * W] = jnp.broadcast_to(gain_ref[i : i + 1, :], (W, W)).T

        @loop(HID // BLOCK)
        def _(i):
            at = pl.ds(pl.multiple_of(i * BLOCK, BLOCK), BLOCK)
            w_in_t[at, :] = w_in[:, at].T
            w_out_t[:, at] = w_out[at, :].T

        wait_bytes(cell_grads.at[pl.ds(0, 3)], cot_recv)
        wait_bytes(cell_grads.at[0], here_sem.at[1])
        upstream = cell_grads[...].reshape(C, W)

        @loop(HID // BLOCK)
        def _(i):
            at = pl.ds(pl.multiple_of(i * BLOCK, BLOCK), BLOCK)
            grad_act[at, :] = jnp.dot(w_out[at, :], upstream, preferred_element_type=F32)


    def row_convolution(wide):
        def tap(t, acc):
            return acc + v_taps[t][None] * wide[pl.ds(t + 1, ROWS)]

        acc = jnp.zeros((ROWS, GROUP, W), F32)
        for t in range(K):
            acc = tap(t, acc)
        return acc

    @pl.when(works)
    def _():
        wait_halo(tall_s, 0)
        wide_s[...] = tall_s[...].astype(F32)
        mixed[...] = row_convolution(wide_s).astype(BF16)

        @loop(ROWS)
        def _(r):
            go(
                jnp.logical_and(points, r == my_row),
                mixed.at[r],
                cell_values.at[y * GROUPS + place],
                mix_send,
                mix_recv,
                here_sem.at[3],
                level + r // 2,
                r % COUNT_Y,
            )

        wait_bytes(tall_f.at[pl.ds(HALO, 14)], rows_recv.at[PLACES])
        wait_bytes(tall_f.at[pl.ds(HALO, 2)], here_sem.at[2])
        send_halo(tall_f, 1)

    @pl.when(points)
    def _():
        @pl.when(works)
        def _():
            wait_bytes(cell_values.at[pl.ds(0, C // GROUP - 1)], mix_recv)
            wait_bytes(cell_values.at[0], here_sem.at[3])

        @pl.when(idles)
        def _():
            wait_bytes(cell_values, mix_recv)

        values = cell_values[...].reshape(C, W).astype(F32)
        centred = values - jnp.sum(values, axis=0, keepdims=True) * (1.0 / C)
        variance = jnp.sum(centred * centred, axis=0, keepdims=True) * (1.0 / C)
        inverse = lax.rsqrt(variance + EPSILON)
        scaled = centred * inverse
        standard[...] = scaled
        inverse_rows[...] = inverse
        normed[...] = (scaled * gain[...]).astype(BF16)

        @loop(HID // BLOCK)
        def _(i):
            at = pl.ds(pl.multiple_of(i * BLOCK, BLOCK), BLOCK)
            pre = jnp.dot(w_in_t[at, :], normed[...], preferred_element_type=F32)
            cumulative = 0.5 * (1.0 + lax.erf(pre * ROOT_HALF))
            activated[at, :] = (pre * cumulative).astype(BF16)
            density = jnp.exp(-0.5 * pre * pre) * INV_ROOT_TWO_PI
            grad_pre[at, :] = (grad_act[at, :] * (cumulative + pre * density)).astype(BF16)

        scaled = jnp.dot(w_in[...], grad_pre[...], preferred_element_type=F32) * gain[...]
        mean_scaled = jnp.sum(scaled, axis=0, keepdims=True) * (1.0 / C)
        mean_product = jnp.sum(scaled * standard[...], axis=0, keepdims=True) * (1.0 / C)
        back = (scaled - mean_scaled - standard[...] * mean_product) * inverse_rows[...]
        grad_cells[...] = back.astype(BF16).reshape(C // GROUP, GROUP, W)

        @loop(C // GROUP)
        def _(i):
            to_y = i // GROUPS
            to_place = i % GROUPS
            go(
                jnp.logical_and(to_y == y, to_place == place),
                grad_cells.at[i],
                grad_rows.at[my_row],
                back_send,
                back_recv,
                here_sem.at[4],
                level + to_place,
                to_y,
            )

        branch = jnp.dot(w_out_t[...], activated[...], preferred_element_type=F32)
        branch_cells[...] = branch.astype(BF16).reshape(COUNT_Y, LOCAL, W)

        @loop(COUNT_Y)
        def _(i):
            go(
                i == y,
                branch_cells.at[i],
                branch_rows.at[y % 2],
                branch_send,
                branch_recv,
                here_sem.at[5],
                band,
                i,
            )


    lane = lax.broadcasted_iota(jnp.int32, (GROUP, W), 1)

    @pl.when(works)
    def _():
        pl.semaphore_wait(far_sem.at[0], 2)
        tell(far_sem.at[1], 4)
        tell(far_sem.at[1], -4)
        wait_halo(tall_f, 1)
        wide_f[...] = tall_f[...].astype(F32)
        rows_f = row_convolution(wide_f)
        column = lax.broadcasted_iota(jnp.int32, (ROWS * GROUP, W), 1)
        rows_f = rows_f.reshape(ROWS * GROUP, W)

        @loop(K)
        def _(t):
            moved = pltpu.roll(rows_f, lax.rem(W + RADIUS - t, W), 1)
            first = column + (t - RADIUS)
            moved = jnp.where(jnp.logical_and(first >= 0, first < W), moved, 0.0)
            shifted[t] = moved.reshape(ROWS, GROUP, W)

        @pl.when(points)
        def _():
            wait_bytes(grad_rows.at[pl.ds(0, ROWS - 1)], back_recv)
            wait_bytes(grad_rows.at[0], here_sem.at[4])

        @pl.when(rests)
        def _():
            wait_bytes(grad_rows, back_recv)

        grads = grad_rows[...].astype(F32)

        def tap(t, sums):
            v_sum = jnp.sum(grads * wide_s[pl.ds(t + 1, ROWS)], axis=0)
            h_sum = jnp.sum(grads * shifted[t], axis=0)
            sums = jnp.where(lane == t, jnp.sum(v_sum, axis=1, keepdims=True), sums)
            return jnp.where(lane == t + 64, jnp.sum(h_sum, axis=1, keepdims=True), sums)

        sums = jnp.zeros((GROUP, W), F32)
        for t in range(K):
            sums = tap(t, sums)
        partial[...] = sums.astype(BF16)
        partials[z] = sums.astype(BF16)
        pl.semaphore_wait(far_sem.at[1], 2)

        @loop(LEVELS)
        def _(i):
            @pl.when(i != z)
            def _():
                remote(
                    partial,
                    partials.at[z],
                    sum_send,
                    sum_recv,
                    i * PLACES + place,
                    y,
                ).start()


    @pl.when(points)
    def _():
        wait_bytes(branch_rows.at[0], branch_recv)
        wait_bytes(branch_rows.at[0], here_sem.at[5])

    @pl.when(rests)
    def _():
        wait_bytes(branch_rows, branch_recv)

    for row in range(2):
        added = f_rows[:, row].reshape(LOCAL, W).astype(F32) + branch_rows[row].astype(F32)
        out_rows[row] = added.astype(BF16)
    store_out = pltpu.make_async_copy(out_rows, out_hbm, here_sem.at[6])
    store_out.start()

    @pl.when(works)
    def _():
        wait_bytes(partials.at[pl.ds(0, LEVELS - 1)], sum_recv)
        grads = jnp.sum(partials[...].astype(F32), axis=0)
        squares = jnp.sum(grads * grads, axis=1, keepdims=True) / (2 * K)
        steps = STEP_SIZE * grads * lax.rsqrt(squares + EPSILON)
        update[...] = steps
        pltpu.make_async_copy(update, updates.at[place], here_sem.at[7]).start()

        @loop(PLACES)
        def _(i):
            @pl.when(i != place)
            def _():
                remote(
                    update,
                    updates.at[place],
                    all_send,
                    all_recv,
                    level + i,
                    y,
                ).start()

        wait_bytes(updates.at[pl.ds(0, GROUPS - 1)], all_recv)

    @pl.when(idles)
    def _():
        wait_bytes(updates.at[pl.ds(0, GROUPS)], all_recv)

    store_out.wait()

    @pl.when(works)
    def _():
        for which, tall in enumerate((tall_s, tall_f)):
            wait_bytes(tall.at[pl.ds(0, 10)], rows_send.at[which])
            for m, (step, here, there, rows) in enumerate(moves):

                @pl.when(inside(step))
                def _(m=m, tall=tall, which=which, here=here, rows=rows):
                    wait_bytes(tall.at[pl.ds(here, rows)], halo_send.at[which, m])

        @pl.when(points)
        def _():
            wait_bytes(mixed.at[pl.ds(0, ROWS - 1)], mix_send)
            wait_bytes(grad_cells.at[pl.ds(0, C // GROUP - 1)], back_send)

        @pl.when(rests)
        def _():
            wait_bytes(mixed, mix_send)

        wait_bytes(partials.at[pl.ds(0, LEVELS - 1)], sum_send)
        wait_bytes(updates.at[pl.ds(0, PLACES - 1)], all_send)
        wait_bytes(update, here_sem.at[7])

    @pl.when(idles)
    def _():
        for which, tall in enumerate((tall_s, tall_f)):
            wait_bytes(tall.at[pl.ds(0, 12)], rows_send.at[which])

        @pl.when(points)
        def _():
            wait_bytes(grad_cells, back_send)

    @pl.when(points)
    def _():
        wait_bytes(cell_grads.at[0], cot_send)
        wait_bytes(branch_cells.at[pl.ds(0, COUNT_Y - 1)], branch_send)

    @pl.when(rests)
    def _():
        wait_bytes(cell_grads.at[pl.ds(0, 2)], cot_send)


def finish(
    out_rows, step_ref, h_ref, v_ref, h_avg, v_avg, out_ref, h_new, v_new, h_swa, v_swa
):
    for row in range(2):
        out_ref[:, row, :] = out_rows[row]
    steps = step_ref[...].reshape(W, W).T
    new = h_ref[...] - steps[64 : 64 + K, 0:LOCAL]
    h_new[...] = new
    h_swa[...] = (AVERAGED * h_avg[...] + new) / (AVERAGED + 1)
    new = v_ref[...] - steps[0:K, 0:LOCAL]
    v_new[...] = new
    v_swa[...] = (AVERAGED * v_avg[...] + new) / (AVERAGED + 1)


def local(
    features,
    h_kernel,
    v_kernel,
    h_kernel_avg,
    v_kernel_avg,
    norm_gain,
    w_in,
    w_out,
    cotangent,
    tissue,
):
    vmem = pl.BlockSpec(memory_space=pltpu.VMEM)
    hbm = pl.BlockSpec(memory_space=pl.ANY)
    dma = pltpu.SemaphoreType.DMA
    out, step = pl.pallas_call(
        kernel,
        name="swa_step",
        out_shape=(
            jax.ShapeDtypeStruct((2, LOCAL, W), BF16),
            jax.ShapeDtypeStruct((PLACES, GROUP, W), F32),
        ),
        in_specs=[hbm] * 8,
        out_specs=(hbm, hbm),
        scratch_shapes=[
            pltpu.VMEM((2, W), jnp.int32),
            pltpu.VMEM((K, LOCAL), F32),
            pltpu.VMEM((K, LOCAL), F32),
            pltpu.VMEM((C // W, W), F32),
            pltpu.VMEM((2, LOCAL, W), BF16),
            pltpu.VMEM((LOCAL, 2, W), BF16),
            pltpu.VMEM((LOCAL, 2, W), BF16),
            pltpu.VMEM((GROUPS, 2, GROUP, W), BF16),
            pltpu.VMEM((2, LOCAL, W), BF16),
            pltpu.VMEM((C, HID), BF16),
            pltpu.VMEM((HID, C), BF16),
            pltpu.VMEM((HID, C), BF16),
            pltpu.VMEM((C, HID), BF16),
            pltpu.VMEM((C, W), F32),
            pltpu.VMEM((2, W, W), F32),
            pltpu.VMEM((GROUPS, 2, GROUP, W), BF16),
            pltpu.VMEM((TALL, GROUP, W), BF16),
            pltpu.VMEM((TALL, GROUP, W), BF16),
            pltpu.VMEM((TALL, GROUP, W), F32),
            pltpu.VMEM((TALL, GROUP, W), F32),
            pltpu.VMEM((K, GROUP, W), F32),
            pltpu.VMEM((K, ROWS, GROUP, W), F32),
            pltpu.VMEM((ROWS, GROUP, W), BF16),
            pltpu.VMEM((COUNT_Y, LOCAL, W), BF16),
            pltpu.VMEM((HID, W), F32),
            pltpu.VMEM((C // GROUP, GROUP, W), BF16),
            pltpu.VMEM((C, W), F32),
            pltpu.VMEM((1, W), F32),
            pltpu.VMEM((C, W), BF16),
            pltpu.VMEM((HID, W), BF16),
            pltpu.VMEM((HID, W), BF16),
            pltpu.VMEM((C // GROUP, GROUP, W), BF16),
            pltpu.VMEM((ROWS, GROUP, W), BF16),
            pltpu.VMEM((COUNT_Y, LOCAL, W), BF16),
            pltpu.VMEM((2, LOCAL, W), BF16),
            pltpu.VMEM((GROUP, W), BF16),
            pltpu.VMEM((LEVELS, GROUP, W), BF16),
            pltpu.VMEM((GROUP, W), F32),
            pltpu.SemaphoreType.REGULAR((3,)),
            dma((8,)),
            dma((8,)),
            dma((2,)),
            dma((PLACES + 1,)),
            dma((2, 4)),
            dma((2, 4)),
            dma,
            dma,
            dma,
            dma,
            dma,
            dma,
            dma,
            dma,
            dma,
            dma,
            dma,
            dma,
        ],
        compiler_params=pltpu.CompilerParams(collective_id=0, has_side_effects=True),
    )(
        features,
        cotangent,
        tissue,
        h_kernel.T,
        v_kernel.T,
        norm_gain.reshape(C // W, W),
        w_in,
        w_out,
    )
    taps = jax.ShapeDtypeStruct((K, LOCAL), F32)
    block_out, h_new, v_new, h_swa, v_swa = pl.pallas_call(
        finish,
        name="finish",
        out_shape=(jax.ShapeDtypeStruct((LOCAL, 2, W), BF16), taps, taps, taps, taps),
        in_specs=[vmem] * 6,
        out_specs=(vmem,) * 5,
    )(out, step, h_kernel.T, v_kernel.T, h_kernel_avg.T, v_kernel_avg.T)
    return (block_out, h_new.T, v_new.T, h_swa.T, v_swa.T)


def solution(mesh):
    return jax.shard_map(
        local,
        mesh=mesh,
        in_specs=(
            P("chan", "band", None),
            P("chan", None),
            P("chan", None),
            P("chan", None),
            P("chan", None),
            P(),
            P(),
            P(),
            P("chan", "band", None),
            P("band", None),
        ),
        out_specs=(
            P("chan", "band", None),
            P("chan", None),
            P("chan", None),
            P("chan", None),
            P("chan", None),
        ),
        check_vma=False,
    )
```

```python
import math

import jax
import jax.numpy as jnp
from jax import lax
from jax.experimental import pallas as pl
from jax.experimental.pallas import tpu as pltpu
from jax.sharding import PartitionSpec as P

AVERAGED = 4
EPSILON = 1e-06
STEP_SIZE = 0.1
ROOT_HALF = math.sqrt(0.5)
INV_ROOT_TWO_PI = 1.0 / math.sqrt(2.0 * math.pi)

MESH = pl.DeviceIdType.MESH
BF16 = jnp.bfloat16
F32 = jnp.float32

PLACES = 8
LEVELS = 16
COUNT_Y = 4
ROWS = 2 * PLACES
GROUPS = 6
GROUP = 16
LOCAL = GROUPS * GROUP
C = COUNT_Y * LOCAL
HID = 1536
K = 47
RADIUS = 23
W = 128
HALO = 24
TALL = ROWS + 2 * HALO
BLOCK = 256


def wait_bytes(view, sem):
    pltpu.make_async_copy(view, view, sem).wait()


def kernel(
    f_hbm,
    cot_hbm,
    tissue_hbm,
    h_hbm,
    v_hbm,
    gain_hbm,
    w_in_hbm,
    w_out_hbm,
    out_hbm,
    updates,
    tissue_ref,
    h_ref,
    v_ref,
    gain_ref,
    out_rows,
    f_pairs,
    cot_pairs,
    f_rows,
    w_rows,
    w_in,
    w_out,
    w_in_t,
    w_out_t,
    gain,
    taps,
    pads,
    smoothed,
    tall_s,
    tall_f,
    wide_s,
    matrix,
    masked,
    mixed,
    cell_grads,
    grad_act,
    cell_values,
    standard,
    inverse_rows,
    normed,
    activated,
    grad_pre,
    grad_cells,
    grad_rows,
    branch_cells,
    branch_rows,
    partial,
    partials,
    update,
    far_sem,
    load_sem,
    here_sem,
    rows_send,
    rows_recv,
    halo_send,
    halo_recv,
    cot_send,
    cot_recv,
    mix_send,
    mix_recv,
    back_send,
    back_recv,
    branch_send,
    branch_recv,
    sum_send,
    sum_recv,
    all_send,
    all_recv,
):
    band = lax.axis_index("band")
    y = lax.axis_index("chan")
    z = band // PLACES
    place = band % PLACES
    core = band % 2
    works = place < GROUPS
    idles = place >= GROUPS
    points = core == y // 2
    rests = core != y // 2
    my_row = 2 * place + y % 2
    level = z * PLACES

    def remote(src, dst, send, recv, to_band, to_y):
        return pltpu.make_async_remote_copy(
            src_ref=src,
            dst_ref=dst,
            send_sem=send,
            recv_sem=recv,
            device_id=(to_band, to_y),
            device_id_type=MESH,
        )

    def go(stays, src, dst, send, recv, here, to_band, to_y):
        @pl.when(stays)
        def _():
            pltpu.make_async_copy(src, dst, here).start()

        @pl.when(jnp.logical_not(stays))
        def _():
            remote(src, dst, send, recv, to_band, to_y).start()

    def loop(count):
        return lambda body: [body(i) for i in range(count)]

    load_in = pltpu.make_async_copy(w_in_hbm, w_in, load_sem.at[0])
    load_out = pltpu.make_async_copy(w_out_hbm, w_out, load_sem.at[1])
    load_f = pltpu.make_async_copy(f_hbm, f_pairs, load_sem.at[2])
    load_cot = pltpu.make_async_copy(cot_hbm, cot_pairs, load_sem.at[3])
    small = [
        pltpu.make_async_copy(src, dst, load_sem.at[4 + i])
        for i, (src, dst) in enumerate(
            ((h_hbm, h_ref), (v_hbm, v_ref), (tissue_hbm, tissue_ref), (gain_hbm, gain_ref))
        )
    ]
    for load in (load_f, *small, load_cot, load_in, load_out):
        load.start()

    barrier = pltpu.get_barrier_semaphore()

    for step in range(1, PLACES):
        line = level + lax.rem(place + step, PLACES)
        pl.semaphore_signal(barrier, 1, device_id=(line, y), device_id_type=MESH)
    others = [lax.rem(y + step, COUNT_Y) for step in range(1, COUNT_Y)]
    for to_y in others:
        pl.semaphore_signal(barrier, 1, device_id=(band, to_y), device_id_type=MESH)

    def tell(sem, step):
        there = lax.rem(z + step + LEVELS, LEVELS)
        pl.semaphore_signal(
            sem, 1, device_id=(there * PLACES + place, y), device_id_type=MESH
        )

    @pl.when(works)
    def _():
        for step in (1, -1, 2, -2):
            tell(barrier, step)

    pads[:, 0:HALO] = jnp.zeros((2, HALO, W), F32)
    pads[:, HALO + W :] = jnp.zeros((2, HALO, W), F32)
    small[0].wait()
    h_ref[...] = h_ref[...].astype(BF16).astype(F32)
    load_f.wait()
    for row in range(2):
        source = f_pairs[:, row, :].astype(F32)
        f_rows[:, row] = source.astype(BF16).reshape(GROUPS, GROUP, W)
        pads[row, HALO : HALO + W, 0:LOCAL] = source.T
    sums = [jnp.zeros((W, LOCAL), F32) for row in range(2)]
    for t in range(K):
        weight = h_ref[t : t + 1, :]
        for row in range(2):
            sums[row] = sums[row] + weight * pads[row, t + 1 : t + 1 + W, 0:LOCAL]
    for row in range(2):
        smoothed[:, row] = sums[row].T.astype(BF16).reshape(GROUPS, GROUP, W)

    @pl.when(works)
    def _():
        pl.semaphore_wait(barrier, PLACES - 1 + COUNT_Y - 1 + 4)
        tell(far_sem.at[0], 2)
        tell(far_sem.at[0], -2)

    @pl.when(idles)
    def _():
        pl.semaphore_wait(barrier, PLACES - 1 + COUNT_Y - 1)

    for to_y in others:
        pl.semaphore_signal(far_sem.at[2], 1, device_id=(band, to_y), device_id_type=MESH)

    own_pair = pl.ds(HALO + 2 * place, 2)

    @loop(GROUPS)
    def _(g):
        go(
            g == place,
            smoothed.at[g],
            tall_s.at[own_pair],
            rows_send.at[0],
            rows_recv.at[place],
            here_sem.at[0],
            level + g,
            y,
        )

    for load in small[1:]:
        load.wait()
    load_cot.wait()
    for row in range(2):
        mask = tissue_ref[row : row + 1, :].astype(F32)
        w_rows[row] = (cot_pairs[:, row, :].astype(F32) * mask).astype(BF16)
    for row in range(2):
        go(
            jnp.logical_and(points, y % 2 == row),
            w_rows.at[row],
            cell_grads.at[y],
            cot_send,
            cot_recv,
            here_sem.at[1],
            band,
            2 * core + row,
        )

    @loop(GROUPS)
    def _(g):
        go(
            g == place,
            f_rows.at[g],
            tall_f.at[own_pair],
            rows_send.at[1],
            rows_recv.at[PLACES],
            here_sem.at[2],
            level + g,
            y,
        )

    moves = (
        (1, HALO, 8, ROWS),
        (-1, HALO, HALO + ROWS, ROWS),
        (2, HALO + 8, 0, 8),
        (-2, HALO, HALO + 2 * ROWS, 8),
    )

    def inside(step):
        return jnp.logical_and(z + step >= 0, z + step < LEVELS)

    def send_halo(tall, which):
        for m, (step, here, there, rows) in enumerate(moves):

            @pl.when(inside(step))
            def _(m=m, step=step, here=here, there=there, rows=rows):
                remote(
                    tall.at[pl.ds(here, rows)],
                    tall.at[pl.ds(there, rows)],
                    halo_send.at[which, m],
                    halo_recv.at[which, m],
                    (z + step) * PLACES + place,
                    y,
                ).start()

    def wait_halo(tall, which):
        for m, (step, here, there, rows) in enumerate(moves):

            @pl.when(inside(-step))
            def _(m=m, there=there, rows=rows):
                wait_bytes(tall.at[pl.ds(there, rows)], halo_recv.at[which, m])

            @pl.when(jnp.logical_not(inside(-step)))
            def _(there=there, rows=rows):
                tall[pl.ds(there, rows)] = jnp.zeros((rows, GROUP, W), BF16)

    @pl.when(works)
    def _():
        for hop, flip in ((0, 0), (0, 1), (1, 0), (1, 1), (3, 0), (3, 1), (2, 0), (2, 1)):
            source = lax.rem(place + 2 * hop, PLACES)
            if flip:
                source = source + 1 - 2 * core
            pair = tall_s.at[pl.ds(HALO + 2 * source, 2)]
            if hop == 0 and flip == 0:
                wait_bytes(pair, here_sem.at[0])
            else:
                wait_bytes(pair, rows_recv.at[source])
            upper = source >= PLACES // 2
            far = jnp.where(upper, 2, -2)
            far_row = jnp.where(upper, 2 * source - 8, HALO + 2 * ROWS + 2 * source)
            far_m = jnp.where(upper, 2, 3)
            for m, step, row in (
                (far_m, far, far_row),
                (0, 1, 8 + 2 * source),
                (1, -1, HALO + ROWS + 2 * source),
            ):

                @pl.when(inside(step))
                def _(m=m, step=step, row=row, pair=pair):
                    remote(
                        pair,
                        tall_s.at[pl.ds(row, 2)],
                        halo_send.at[0, m],
                        halo_recv.at[0, m],
                        (z + step) * PLACES + place,
                        y,
                    ).start()

        taps[...] = jnp.zeros((W, W), F32)
        taps[0:K, 0:LOCAL] = v_ref[...]
        taps[...] = taps[...].T
        v_half = taps[pl.ds(pl.multiple_of(place * GROUP, GROUP), GROUP), :].astype(BF16)
        wide_lane = lax.broadcasted_iota(jnp.int32, (W, TALL * GROUP), 1)
        wide_tap = lax.broadcasted_iota(jnp.int32, (W, TALL * GROUP), 0)
        spread = (wide_lane // GROUP == wide_tap).astype(F32).astype(BF16)
        base = jnp.dot(v_half, spread, preferred_element_type=F32)
        group_lane = lax.broadcasted_iota(jnp.int32, (GROUP, TALL * GROUP), 1)
        group_row = lax.broadcasted_iota(jnp.int32, (GROUP, TALL * GROUP), 0)
        base = jnp.where(group_lane % GROUP == group_row, base, 0.0)
        for r in range(ROWS):
            moved = pltpu.roll(base, GROUP * (r + 1), 1)
            matrix[r * GROUP : (r + 1) * GROUP] = moved.astype(BF16)

    load_in.wait()
    load_out.wait()
    pl.semaphore_wait(far_sem.at[2], COUNT_Y - 1)

    @pl.when(points)
    def _():
        for i in range(C // W):
            gain[i * W : (i + 1) * W] = jnp.broadcast_to(gain_ref[i : i + 1, :], (W, W)).T

        @loop(HID // BLOCK)
        def _(i):
            at = pl.ds(pl.multiple_of(i * BLOCK, BLOCK), BLOCK)
            w_in_t[at, :] = w_in[:, at].T
            w_out_t[:, at] = w_out[at, :].T

        wait_bytes(cell_grads.at[pl.ds(0, 3)], cot_recv)
        wait_bytes(cell_grads.at[0], here_sem.at[1])
        upstream = cell_grads[...].reshape(C, W)

        @loop(HID // BLOCK)
        def _(i):
            at = pl.ds(pl.multiple_of(i * BLOCK, BLOCK), BLOCK)
            grad_act[at, :] = jnp.dot(w_out[at, :], upstream, preferred_element_type=F32)


    def row_convolution(tall):
        flat = tall[...].reshape(TALL * GROUP, W)
        return jnp.dot(matrix[...], flat, preferred_element_type=F32)

    @pl.when(works)
    def _():
        wait_halo(tall_s, 0)
        mixed[...] = row_convolution(tall_s).astype(BF16).reshape(ROWS, GROUP, W)

        @loop(ROWS)
        def _(r):
            go(
                jnp.logical_and(points, r == my_row),
                mixed.at[r],
                cell_values.at[y * GROUPS + place],
                mix_send,
                mix_recv,
                here_sem.at[3],
                level + r // 2,
                r % COUNT_Y,
            )

        wait_bytes(tall_f.at[pl.ds(HALO, 14)], rows_recv.at[PLACES])
        wait_bytes(tall_f.at[pl.ds(HALO, 2)], here_sem.at[2])
        send_halo(tall_f, 1)

    @pl.when(points)
    def _():
        @pl.when(works)
        def _():
            wait_bytes(cell_values.at[pl.ds(0, C // GROUP - 1)], mix_recv)
            wait_bytes(cell_values.at[0], here_sem.at[3])

        @pl.when(idles)
        def _():
            wait_bytes(cell_values, mix_recv)

        values = cell_values[...].reshape(C, W).astype(F32)
        centred = values - jnp.sum(values, axis=0, keepdims=True) * (1.0 / C)
        variance = jnp.sum(centred * centred, axis=0, keepdims=True) * (1.0 / C)
        inverse = lax.rsqrt(variance + EPSILON)
        scaled = centred * inverse
        standard[...] = scaled
        inverse_rows[...] = inverse
        normed[...] = (scaled * gain[...]).astype(BF16)

        @loop(HID // BLOCK)
        def _(i):
            at = pl.ds(pl.multiple_of(i * BLOCK, BLOCK), BLOCK)
            pre = jnp.dot(w_in_t[at, :], normed[...], preferred_element_type=F32)
            cumulative = 0.5 * (1.0 + lax.erf(pre * ROOT_HALF))
            activated[at, :] = (pre * cumulative).astype(BF16)
            density = jnp.exp(-0.5 * pre * pre) * INV_ROOT_TWO_PI
            grad_pre[at, :] = (grad_act[at, :] * (cumulative + pre * density)).astype(BF16)

        scaled = jnp.dot(w_in[...], grad_pre[...], preferred_element_type=F32) * gain[...]
        mean_scaled = jnp.sum(scaled, axis=0, keepdims=True) * (1.0 / C)
        mean_product = jnp.sum(scaled * standard[...], axis=0, keepdims=True) * (1.0 / C)
        back = (scaled - mean_scaled - standard[...] * mean_product) * inverse_rows[...]
        grad_cells[...] = back.astype(BF16).reshape(C // GROUP, GROUP, W)

        @loop(C // GROUP)
        def _(i):
            to_y = i // GROUPS
            to_place = i % GROUPS
            go(
                jnp.logical_and(to_y == y, to_place == place),
                grad_cells.at[i],
                grad_rows.at[my_row],
                back_send,
                back_recv,
                here_sem.at[4],
                level + to_place,
                to_y,
            )

        branch = jnp.dot(w_out_t[...], activated[...], preferred_element_type=F32)
        branch_cells[...] = branch.astype(BF16).reshape(COUNT_Y, LOCAL, W)

        @loop(COUNT_Y)
        def _(i):
            go(
                i == y,
                branch_cells.at[i],
                branch_rows.at[y % 2],
                branch_send,
                branch_recv,
                here_sem.at[5],
                band,
                i,
            )


    lane = lax.broadcasted_iota(jnp.int32, (GROUP, W), 1)

    @pl.when(works)
    def _():
        pl.semaphore_wait(far_sem.at[0], 2)
        tell(far_sem.at[1], 4)
        tell(far_sem.at[1], -4)
        wait_halo(tall_f, 1)
        wide_s[...] = tall_s[...].astype(F32)
        rows_f = row_convolution(tall_f).astype(BF16)
        first = lax.broadcasted_iota(jnp.int32, (W, W), 0)
        second = lax.broadcasted_iota(jnp.int32, (W, W), 1)
        mirror = (first + second == W - 1).astype(F32).astype(BF16)
        turned = lax.dot_general(
            mirror, rows_f, (((1,), (1,)), ((), ())), preferred_element_type=F32
        )
        channel = lax.broadcasted_iota(jnp.int32, (W, ROWS * GROUP), 1) % GROUP
        for c in range(GROUP):
            kept = jnp.where(channel == c, turned, 0.0)
            masked[c * W : (c + 1) * W] = kept.astype(BF16)
        @pl.when(points)
        def _():
            wait_bytes(grad_rows.at[pl.ds(0, ROWS - 1)], back_recv)
            wait_bytes(grad_rows.at[0], here_sem.at[4])

        @pl.when(rests)
        def _():
            wait_bytes(grad_rows, back_recv)

        flat = grad_rows[...].reshape(ROWS * GROUP, W)
        near = jnp.abs(first + second - (W - 1)) <= RADIUS
        h_sums = []
        for part in range(4):
            at = pl.ds(part * 4 * W, 4 * W)
            pairs = jnp.dot(masked[at, :], flat, preferred_element_type=F32)
            for c in range(4):
                block = jnp.where(near, pairs[c * W : (c + 1) * W], 0.0)
                block = pltpu.roll(block, 0, 1, stride=1, stride_axis=0)
                h_sums.append(jnp.sum(block, axis=0, keepdims=True))
        sums = jnp.concatenate(h_sums, axis=0)
        grads = grad_rows[...].astype(F32)
        for t in range(K):
            v_sum = jnp.sum(grads * wide_s[pl.ds(t + 1, ROWS)], axis=0)
            sums = jnp.where(lane == t + 32, jnp.sum(v_sum, axis=1, keepdims=True), sums)
        partial[...] = sums.astype(BF16)
        partials[z] = sums.astype(BF16)
        pl.semaphore_wait(far_sem.at[1], 2)

        @loop(LEVELS)
        def _(i):
            @pl.when(i != z)
            def _():
                remote(
                    partial,
                    partials.at[z],
                    sum_send,
                    sum_recv,
                    i * PLACES + place,
                    y,
                ).start()


    @pl.when(points)
    def _():
        wait_bytes(branch_rows.at[0], branch_recv)
        wait_bytes(branch_rows.at[0], here_sem.at[5])

    @pl.when(rests)
    def _():
        wait_bytes(branch_rows, branch_recv)

    for row in range(2):
        added = f_rows[:, row].reshape(LOCAL, W).astype(F32) + branch_rows[row].astype(F32)
        out_rows[row] = added.astype(BF16)
    store_out = pltpu.make_async_copy(out_rows, out_hbm, here_sem.at[6])
    store_out.start()

    @pl.when(works)
    def _():
        wait_bytes(partials.at[pl.ds(0, LEVELS - 1)], sum_recv)
        grads = jnp.sum(partials[...].astype(F32), axis=0)
        squares = jnp.sum(grads * grads, axis=1, keepdims=True) / (2 * K)
        steps = STEP_SIZE * grads * lax.rsqrt(squares + EPSILON)
        update[...] = steps.astype(BF16)
        pltpu.make_async_copy(update, updates.at[place], here_sem.at[7]).start()

        @loop(PLACES)
        def _(i):
            @pl.when(i != place)
            def _():
                remote(
                    update,
                    updates.at[place],
                    all_send,
                    all_recv,
                    level + i,
                    y,
                ).start()

        wait_bytes(updates.at[pl.ds(0, GROUPS - 1)], all_recv)

    @pl.when(idles)
    def _():
        wait_bytes(updates.at[pl.ds(0, GROUPS)], all_recv)

    store_out.wait()

    @pl.when(works)
    def _():
        for which, tall in enumerate((tall_s, tall_f)):
            wait_bytes(tall.at[pl.ds(0, 10)], rows_send.at[which])
            for m, (step, here, there, rows) in enumerate(moves):

                @pl.when(inside(step))
                def _(m=m, tall=tall, which=which, here=here, rows=rows):
                    wait_bytes(tall.at[pl.ds(here, rows)], halo_send.at[which, m])

        @pl.when(points)
        def _():
            wait_bytes(mixed.at[pl.ds(0, ROWS - 1)], mix_send)
            wait_bytes(grad_cells.at[pl.ds(0, C // GROUP - 1)], back_send)

        @pl.when(rests)
        def _():
            wait_bytes(mixed, mix_send)

        wait_bytes(partials.at[pl.ds(0, LEVELS - 1)], sum_send)
        wait_bytes(updates.at[pl.ds(0, PLACES - 1)], all_send)
        wait_bytes(update, here_sem.at[7])

    @pl.when(idles)
    def _():
        for which, tall in enumerate((tall_s, tall_f)):
            wait_bytes(tall.at[pl.ds(0, 12)], rows_send.at[which])

        @pl.when(points)
        def _():
            wait_bytes(grad_cells, back_send)

    @pl.when(points)
    def _():
        wait_bytes(cell_grads.at[0], cot_send)
        wait_bytes(branch_cells.at[pl.ds(0, COUNT_Y - 1)], branch_send)

    @pl.when(rests)
    def _():
        wait_bytes(cell_grads.at[pl.ds(0, 2)], cot_send)


def finish(
    out_rows, step_ref, h_ref, v_ref, h_avg, v_avg, out_ref, h_new, v_new, h_swa, v_swa
):
    for row in range(2):
        out_ref[:, row, :] = out_rows[row]
    row = lax.broadcasted_iota(jnp.int32, (W, W), 0)
    lane = lax.broadcasted_iota(jnp.int32, (W, W), 1)
    from_v = jnp.logical_and(row < K, lane == row + 32)
    from_h = jnp.logical_and(row >= 64, lane == (214 - row) % W)
    order = jnp.logical_or(from_v, from_h).astype(F32).astype(BF16)
    steps = lax.dot_general(
        order,
        step_ref[...].reshape(W, W),
        (((1,), (1,)), ((), ())),
        preferred_element_type=F32,
    )
    new = h_ref[...] - steps[64 : 64 + K, 0:LOCAL]
    h_new[...] = new
    h_swa[...] = (AVERAGED * h_avg[...] + new) / (AVERAGED + 1)
    new = v_ref[...] - steps[0:K, 0:LOCAL]
    v_new[...] = new
    v_swa[...] = (AVERAGED * v_avg[...] + new) / (AVERAGED + 1)


def local(
    features,
    h_kernel,
    v_kernel,
    h_kernel_avg,
    v_kernel_avg,
    norm_gain,
    w_in,
    w_out,
    cotangent,
    tissue,
):
    vmem = pl.BlockSpec(memory_space=pltpu.VMEM)
    hbm = pl.BlockSpec(memory_space=pl.ANY)
    dma = pltpu.SemaphoreType.DMA
    out, step = pl.pallas_call(
        kernel,
        name="swa_step",
        out_shape=(
            jax.ShapeDtypeStruct((2, LOCAL, W), BF16),
            jax.ShapeDtypeStruct((PLACES, GROUP, W), BF16),
        ),
        in_specs=[hbm] * 8,
        out_specs=(hbm, hbm),
        scratch_shapes=[
            pltpu.VMEM((2, W), jnp.int32),
            pltpu.VMEM((K, LOCAL), F32),
            pltpu.VMEM((K, LOCAL), F32),
            pltpu.VMEM((C // W, W), F32),
            pltpu.VMEM((2, LOCAL, W), BF16),
            pltpu.VMEM((LOCAL, 2, W), BF16),
            pltpu.VMEM((LOCAL, 2, W), BF16),
            pltpu.VMEM((GROUPS, 2, GROUP, W), BF16),
            pltpu.VMEM((2, LOCAL, W), BF16),
            pltpu.VMEM((C, HID), BF16),
            pltpu.VMEM((HID, C), BF16),
            pltpu.VMEM((HID, C), BF16),
            pltpu.VMEM((C, HID), BF16),
            pltpu.VMEM((C, W), F32),
            pltpu.VMEM((W, W), F32),
            pltpu.VMEM((2, W + 2 * HALO, W), F32),
            pltpu.VMEM((GROUPS, 2, GROUP, W), BF16),
            pltpu.VMEM((TALL, GROUP, W), BF16),
            pltpu.VMEM((TALL, GROUP, W), BF16),
            pltpu.VMEM((TALL, GROUP, W), F32),
            pltpu.VMEM((ROWS * GROUP, TALL * GROUP), BF16),
            pltpu.VMEM((GROUP * W, ROWS * GROUP), BF16),
            pltpu.VMEM((ROWS, GROUP, W), BF16),
            pltpu.VMEM((COUNT_Y, LOCAL, W), BF16),
            pltpu.VMEM((HID, W), F32),
            pltpu.VMEM((C // GROUP, GROUP, W), BF16),
            pltpu.VMEM((C, W), F32),
            pltpu.VMEM((1, W), F32),
            pltpu.VMEM((C, W), BF16),
            pltpu.VMEM((HID, W), BF16),
            pltpu.VMEM((HID, W), BF16),
            pltpu.VMEM((C // GROUP, GROUP, W), BF16),
            pltpu.VMEM((ROWS, GROUP, W), BF16),
            pltpu.VMEM((COUNT_Y, LOCAL, W), BF16),
            pltpu.VMEM((2, LOCAL, W), BF16),
            pltpu.VMEM((GROUP, W), BF16),
            pltpu.VMEM((LEVELS, GROUP, W), BF16),
            pltpu.VMEM((GROUP, W), BF16),
            pltpu.SemaphoreType.REGULAR((3,)),
            dma((8,)),
            dma((8,)),
            dma((2,)),
            dma((PLACES + 1,)),
            dma((2, 4)),
            dma((2, 4)),
            dma,
            dma,
            dma,
            dma,
            dma,
            dma,
            dma,
            dma,
            dma,
            dma,
            dma,
            dma,
        ],
        compiler_params=pltpu.CompilerParams(collective_id=0, has_side_effects=True),
    )(
        features,
        cotangent,
        tissue,
        h_kernel.T,
        v_kernel.T,
        norm_gain.reshape(C // W, W),
        w_in,
        w_out,
    )
    taps = jax.ShapeDtypeStruct((K, LOCAL), F32)
    block_out, h_new, v_new, h_swa, v_swa = pl.pallas_call(
        finish,
        name="finish",
        out_shape=(jax.ShapeDtypeStruct((LOCAL, 2, W), BF16), taps, taps, taps, taps),
        in_specs=[vmem] * 6,
        out_specs=(vmem,) * 5,
    )(out, step, h_kernel.T, v_kernel.T, h_kernel_avg.T, v_kernel_avg.T)
    return (block_out, h_new.T, v_new.T, h_swa.T, v_swa.T)


def solution(mesh):
    return jax.shard_map(
        local,
        mesh=mesh,
        in_specs=(
            P("chan", "band", None),
            P("chan", None),
            P("chan", None),
            P("chan", None),
            P("chan", None),
            P(),
            P(),
            P(),
            P("chan", "band", None),
            P("band", None),
        ),
        out_specs=(
            P("chan", "band", None),
            P("chan", None),
            P("chan", None),
            P("chan", None),
            P("chan", None),
        ),
        check_vma=False,
    )
```

```python
import math

import jax
import jax.numpy as jnp
from jax import lax
from jax.experimental import pallas as pl
from jax.experimental.pallas import tpu as pltpu
from jax.sharding import PartitionSpec as P

AVERAGED = 4
EPSILON = 1e-06
STEP_SIZE = 0.1
ROOT_HALF = math.sqrt(0.5)
INV_ROOT_TWO_PI = 1.0 / math.sqrt(2.0 * math.pi)

MESH = pl.DeviceIdType.MESH
BF16 = jnp.bfloat16
F32 = jnp.float32

PLACES = 8
LEVELS = 16
COUNT_Y = 4
ROWS = 2 * PLACES
GROUPS = 6
GROUP = 16
LOCAL = GROUPS * GROUP
C = COUNT_Y * LOCAL
HID = 1536
K = 47
RADIUS = 23
W = 128
HALO = 24
TALL = ROWS + 2 * HALO
BLOCK = 256


def wait_bytes(view, sem):
    pltpu.make_async_copy(view, view, sem).wait()


def kernel(
    f_hbm,
    cot_hbm,
    tissue_hbm,
    h_hbm,
    v_hbm,
    gain_hbm,
    w_in_hbm,
    w_out_hbm,
    out_hbm,
    updates,
    tissue_ref,
    h_ref,
    v_ref,
    gain_ref,
    out_rows,
    f_pairs,
    cot_pairs,
    f_rows,
    w_rows,
    w_in,
    w_out,
    w_in_t,
    w_out_t,
    gain,
    taps,
    pads,
    smoothed,
    tall_s,
    tall_f,
    wide_s,
    matrix,
    masked,
    v_sums,
    mixed,
    cell_grads,
    grad_act,
    cell_values,
    standard,
    inverse_rows,
    normed,
    activated,
    grad_pre,
    grad_cells,
    grad_rows,
    branch_cells,
    branch_rows,
    partial,
    partials,
    update,
    far_sem,
    load_sem,
    here_sem,
    rows_send,
    rows_recv,
    halo_send,
    halo_recv,
    cot_send,
    cot_recv,
    mix_send,
    mix_recv,
    back_send,
    back_recv,
    branch_send,
    branch_recv,
    sum_send,
    sum_recv,
    all_send,
    all_recv,
):
    band = lax.axis_index("band")
    y = lax.axis_index("chan")
    z = band // PLACES
    place = band % PLACES
    core = band % 2
    works = place < GROUPS
    idles = place >= GROUPS
    points = core == y // 2
    rests = core != y // 2
    my_row = 2 * place + y % 2
    level = z * PLACES

    def remote(src, dst, send, recv, to_band, to_y):
        return pltpu.make_async_remote_copy(
            src_ref=src,
            dst_ref=dst,
            send_sem=send,
            recv_sem=recv,
            device_id=(to_band, to_y),
            device_id_type=MESH,
        )

    def go(stays, src, dst, send, recv, here, to_band, to_y):
        @pl.when(stays)
        def _():
            pltpu.make_async_copy(src, dst, here).start()

        @pl.when(jnp.logical_not(stays))
        def _():
            remote(src, dst, send, recv, to_band, to_y).start()

    def loop(count):
        return lambda body: [body(i) for i in range(count)]

    load_in = pltpu.make_async_copy(w_in_hbm, w_in, load_sem.at[0])
    load_out = pltpu.make_async_copy(w_out_hbm, w_out, load_sem.at[1])
    load_f = pltpu.make_async_copy(f_hbm, f_pairs, load_sem.at[2])
    load_cot = pltpu.make_async_copy(cot_hbm, cot_pairs, load_sem.at[3])
    small = [
        pltpu.make_async_copy(src, dst, load_sem.at[4 + i])
        for i, (src, dst) in enumerate(
            ((h_hbm, h_ref), (v_hbm, v_ref), (tissue_hbm, tissue_ref), (gain_hbm, gain_ref))
        )
    ]
    for load in (load_f, *small, load_cot, load_in, load_out):
        load.start()

    barrier = pltpu.get_barrier_semaphore()

    for step in range(1, PLACES):
        line = level + lax.rem(place + step, PLACES)
        pl.semaphore_signal(barrier, 1, device_id=(line, y), device_id_type=MESH)
    others = [lax.rem(y + step, COUNT_Y) for step in range(1, COUNT_Y)]
    for to_y in others:
        pl.semaphore_signal(barrier, 1, device_id=(band, to_y), device_id_type=MESH)

    def tell(sem, step):
        there = lax.rem(z + step + LEVELS, LEVELS)
        pl.semaphore_signal(
            sem, 1, device_id=(there * PLACES + place, y), device_id_type=MESH
        )

    @pl.when(works)
    def _():
        for step in (1, -1, 2, -2):
            tell(barrier, step)

    pads[:, 0:HALO] = jnp.zeros((2, HALO, W), F32)
    pads[:, HALO + W :] = jnp.zeros((2, HALO, W), F32)
    small[0].wait()
    h_ref[...] = h_ref[...].astype(BF16).astype(F32)
    load_f.wait()
    for row in range(2):
        source = f_pairs[:, row, :].astype(F32)
        f_rows[:, row] = source.astype(BF16).reshape(GROUPS, GROUP, W)
        pads[row, HALO : HALO + W, 0:LOCAL] = source.T
    sums = [jnp.zeros((W, LOCAL), F32) for row in range(2)]
    for t in range(K):
        weight = h_ref[t : t + 1, :]
        for row in range(2):
            sums[row] = sums[row] + weight * pads[row, t + 1 : t + 1 + W, 0:LOCAL]
    for row in range(2):
        smoothed[:, row] = sums[row].T.astype(BF16).reshape(GROUPS, GROUP, W)

    @pl.when(works)
    def _():
        pl.semaphore_wait(barrier, PLACES - 1 + COUNT_Y - 1 + 4)
        tell(far_sem.at[0], 2)
        tell(far_sem.at[0], -2)

    @pl.when(idles)
    def _():
        pl.semaphore_wait(barrier, PLACES - 1 + COUNT_Y - 1)

    for to_y in others:
        pl.semaphore_signal(far_sem.at[2], 1, device_id=(band, to_y), device_id_type=MESH)

    own_pair = pl.ds(HALO + 2 * place, 2)

    @loop(GROUPS)
    def _(g):
        go(
            g == place,
            smoothed.at[g],
            tall_s.at[own_pair],
            rows_send.at[0],
            rows_recv.at[place],
            here_sem.at[0],
            level + g,
            y,
        )

    for load in small[1:]:
        load.wait()
    load_cot.wait()
    for row in range(2):
        mask = tissue_ref[row : row + 1, :].astype(F32)
        w_rows[row] = (cot_pairs[:, row, :].astype(F32) * mask).astype(BF16)
    for row in range(2):
        go(
            jnp.logical_and(points, y % 2 == row),
            w_rows.at[row],
            cell_grads.at[y],
            cot_send,
            cot_recv,
            here_sem.at[1],
            band,
            2 * core + row,
        )

    @loop(GROUPS)
    def _(g):
        go(
            g == place,
            f_rows.at[g],
            tall_f.at[own_pair],
            rows_send.at[1],
            rows_recv.at[PLACES],
            here_sem.at[2],
            level + g,
            y,
        )

    moves = (
        (1, HALO, 8, ROWS),
        (-1, HALO, HALO + ROWS, ROWS),
        (2, HALO + 8, 0, 8),
        (-2, HALO, HALO + 2 * ROWS, 8),
    )

    def inside(step):
        return jnp.logical_and(z + step >= 0, z + step < LEVELS)

    def send_halo(tall, which):
        for m, (step, here, there, rows) in enumerate(moves):

            @pl.when(inside(step))
            def _(m=m, step=step, here=here, there=there, rows=rows):
                remote(
                    tall.at[pl.ds(here, rows)],
                    tall.at[pl.ds(there, rows)],
                    halo_send.at[which, m],
                    halo_recv.at[which, m],
                    (z + step) * PLACES + place,
                    y,
                ).start()

    def wait_halo(tall, which):
        for m, (step, here, there, rows) in enumerate(moves):

            @pl.when(inside(-step))
            def _(m=m, there=there, rows=rows):
                wait_bytes(tall.at[pl.ds(there, rows)], halo_recv.at[which, m])

            @pl.when(jnp.logical_not(inside(-step)))
            def _(there=there, rows=rows):
                tall[pl.ds(there, rows)] = jnp.zeros((rows, GROUP, W), BF16)

    @pl.when(works)
    def _():
        for hop, flip in ((0, 0), (0, 1), (1, 0), (1, 1), (3, 0), (3, 1), (2, 0), (2, 1)):
            source = lax.rem(place + 2 * hop, PLACES)
            if flip:
                source = source + 1 - 2 * core
            pair = tall_s.at[pl.ds(HALO + 2 * source, 2)]
            if hop == 0 and flip == 0:
                wait_bytes(pair, here_sem.at[0])
            else:
                wait_bytes(pair, rows_recv.at[source])
            upper = source >= PLACES // 2
            far = jnp.where(upper, 2, -2)
            far_row = jnp.where(upper, 2 * source - 8, HALO + 2 * ROWS + 2 * source)
            far_m = jnp.where(upper, 2, 3)
            for m, step, row in (
                (far_m, far, far_row),
                (0, 1, 8 + 2 * source),
                (1, -1, HALO + ROWS + 2 * source),
            ):

                @pl.when(inside(step))
                def _(m=m, step=step, row=row, pair=pair):
                    remote(
                        pair,
                        tall_s.at[pl.ds(row, 2)],
                        halo_send.at[0, m],
                        halo_recv.at[0, m],
                        (z + step) * PLACES + place,
                        y,
                    ).start()

        taps[...] = jnp.zeros((W, W), F32)
        taps[0:K, 0:LOCAL] = v_ref[...]
        taps[...] = taps[...].T
        v_half = taps[pl.ds(pl.multiple_of(place * GROUP, GROUP), GROUP), :].astype(BF16)
        wide_lane = lax.broadcasted_iota(jnp.int32, (W, TALL * GROUP), 1)
        wide_tap = lax.broadcasted_iota(jnp.int32, (W, TALL * GROUP), 0)
        spread = (wide_lane // GROUP == wide_tap).astype(F32).astype(BF16)
        base = jnp.dot(v_half, spread, preferred_element_type=F32)
        group_lane = lax.broadcasted_iota(jnp.int32, (GROUP, TALL * GROUP), 1)
        group_row = lax.broadcasted_iota(jnp.int32, (GROUP, TALL * GROUP), 0)
        base = jnp.where(group_lane % GROUP == group_row, base, 0.0)
        for r in range(ROWS):
            moved = pltpu.roll(base, GROUP * (r + 1), 1)
            matrix[r * GROUP : (r + 1) * GROUP] = moved.astype(BF16)

    load_in.wait()
    load_out.wait()
    pl.semaphore_wait(far_sem.at[2], COUNT_Y - 1)

    @pl.when(points)
    def _():
        for i in range(C // W):
            gain[i * W : (i + 1) * W] = jnp.broadcast_to(gain_ref[i : i + 1, :], (W, W)).T

        @loop(HID // BLOCK)
        def _(i):
            at = pl.ds(pl.multiple_of(i * BLOCK, BLOCK), BLOCK)
            w_in_t[at, :] = w_in[:, at].T
            w_out_t[:, at] = w_out[at, :].T

        wait_bytes(cell_grads.at[pl.ds(0, 3)], cot_recv)
        wait_bytes(cell_grads.at[0], here_sem.at[1])
        upstream = cell_grads[...].reshape(C, W)

        @loop(HID // BLOCK)
        def _(i):
            at = pl.ds(pl.multiple_of(i * BLOCK, BLOCK), BLOCK)
            grad_act[at, :] = jnp.dot(w_out[at, :], upstream, preferred_element_type=F32)


    def row_convolution(tall):
        flat = tall[...].reshape(TALL * GROUP, W)
        return jnp.dot(matrix[...], flat, preferred_element_type=F32)

    @pl.when(works)
    def _():
        wait_halo(tall_s, 0)
        mixed[...] = row_convolution(tall_s).astype(BF16).reshape(ROWS, GROUP, W)

        @loop(ROWS)
        def _(r):
            go(
                jnp.logical_and(points, r == my_row),
                mixed.at[r],
                cell_values.at[y * GROUPS + place],
                mix_send,
                mix_recv,
                here_sem.at[3],
                level + r // 2,
                r % COUNT_Y,
            )

        wait_bytes(tall_f.at[pl.ds(HALO, 14)], rows_recv.at[PLACES])
        wait_bytes(tall_f.at[pl.ds(HALO, 2)], here_sem.at[2])
        send_halo(tall_f, 1)

    @pl.when(points)
    def _():
        @pl.when(works)
        def _():
            wait_bytes(cell_values.at[pl.ds(0, C // GROUP - 1)], mix_recv)
            wait_bytes(cell_values.at[0], here_sem.at[3])

        @pl.when(idles)
        def _():
            wait_bytes(cell_values, mix_recv)

        values = cell_values[...].reshape(C, W).astype(F32)
        centred = values - jnp.sum(values, axis=0, keepdims=True) * (1.0 / C)
        variance = jnp.sum(centred * centred, axis=0, keepdims=True) * (1.0 / C)
        inverse = lax.rsqrt(variance + EPSILON)
        scaled = centred * inverse
        standard[...] = scaled
        inverse_rows[...] = inverse
        normed[...] = (scaled * gain[...]).astype(BF16)

        @loop(HID // BLOCK)
        def _(i):
            at = pl.ds(pl.multiple_of(i * BLOCK, BLOCK), BLOCK)
            pre = jnp.dot(w_in_t[at, :], normed[...], preferred_element_type=F32)
            cumulative = 0.5 * (1.0 + lax.erf(pre * ROOT_HALF))
            activated[at, :] = (pre * cumulative).astype(BF16)
            density = jnp.exp(-0.5 * pre * pre) * INV_ROOT_TWO_PI
            grad_pre[at, :] = (grad_act[at, :] * (cumulative + pre * density)).astype(BF16)

        scaled = jnp.dot(w_in[...], grad_pre[...], preferred_element_type=F32) * gain[...]
        mean_scaled = jnp.sum(scaled, axis=0, keepdims=True) * (1.0 / C)
        mean_product = jnp.sum(scaled * standard[...], axis=0, keepdims=True) * (1.0 / C)
        back = (scaled - mean_scaled - standard[...] * mean_product) * inverse_rows[...]
        grad_cells[...] = back.astype(BF16).reshape(C // GROUP, GROUP, W)

        @loop(C // GROUP)
        def _(i):
            to_y = i // GROUPS
            to_place = i % GROUPS
            go(
                jnp.logical_and(to_y == y, to_place == place),
                grad_cells.at[i],
                grad_rows.at[my_row],
                back_send,
                back_recv.at[place // 2],
                here_sem.at[4],
                level + to_place,
                to_y,
            )

        branch = jnp.dot(w_out_t[...], activated[...], preferred_element_type=F32)
        branch_cells[...] = branch.astype(BF16).reshape(COUNT_Y, LOCAL, W)

        @loop(COUNT_Y)
        def _(i):
            go(
                i == y,
                branch_cells.at[i],
                branch_rows.at[y % 2],
                branch_send,
                branch_recv,
                here_sem.at[5],
                band,
                i,
            )


    lane = lax.broadcasted_iota(jnp.int32, (GROUP, W), 1)

    @pl.when(works)
    def _():
        pl.semaphore_wait(far_sem.at[0], 2)
        tell(far_sem.at[1], 4)
        tell(far_sem.at[1], -4)
        wait_halo(tall_f, 1)
        wide_s[...] = tall_s[...].astype(F32)
        rows_f = row_convolution(tall_f).astype(BF16)
        first = lax.broadcasted_iota(jnp.int32, (W, W), 0)
        second = lax.broadcasted_iota(jnp.int32, (W, W), 1)
        mirror = (first + second == W - 1).astype(F32).astype(BF16)
        turned = lax.dot_general(
            mirror, rows_f, (((1,), (1,)), ((), ())), preferred_element_type=F32
        )
        channel = lax.broadcasted_iota(jnp.int32, (W, ROWS * GROUP), 1) % GROUP
        for c in range(GROUP):
            kept = jnp.where(channel == c, turned, 0.0)
            masked[c * W : (c + 1) * W] = kept.astype(BF16)
        def v_part(group, t):
            rows = grad_rows[pl.ds(4 * group, 4)].astype(F32)
            return jnp.sum(rows * wide_s[pl.ds(4 * group + t + 1, 4)], axis=0)

        for nth, offset in enumerate((0, 1, 3)):
            group = lax.rem(place // 2 + offset, 4)
            if offset == 0:

                @pl.when(points)
                def _(group=group):
                    wait_bytes(grad_rows.at[pl.ds(0, 3)], back_recv.at[group])
                    wait_bytes(grad_rows.at[0], here_sem.at[4])

                @pl.when(rests)
                def _(group=group):
                    wait_bytes(grad_rows.at[pl.ds(0, 4)], back_recv.at[group])

            else:
                wait_bytes(grad_rows.at[pl.ds(0, 4)], back_recv.at[group])
            for t in range(K):
                part = v_part(group, t)
                v_sums[t] = v_sums[t] + part if nth else part
        group = lax.rem(place // 2 + 2, 4)
        wait_bytes(grad_rows.at[pl.ds(0, 4)], back_recv.at[group])

        flat = grad_rows[...].reshape(ROWS * GROUP, W)
        near = jnp.abs(first + second - (W - 1)) <= RADIUS
        h_sums = []
        for part in range(4):
            at = pl.ds(part * 4 * W, 4 * W)
            pairs = jnp.dot(masked[at, :], flat, preferred_element_type=F32)
            for c in range(4):
                block = jnp.where(near, pairs[c * W : (c + 1) * W], 0.0)
                block = pltpu.roll(block, 0, 1, stride=1, stride_axis=0)
                h_sums.append(jnp.sum(block, axis=0, keepdims=True))
        sums = jnp.concatenate(h_sums, axis=0)
        for t in range(K):
            v_sum = v_sums[t] + v_part(group, t)
            sums = jnp.where(lane == t + 32, jnp.sum(v_sum, axis=1, keepdims=True), sums)
        partial[...] = sums.astype(BF16)
        partials[z] = sums.astype(BF16)
        pl.semaphore_wait(far_sem.at[1], 2)

        @loop(LEVELS)
        def _(i):
            @pl.when(i != z)
            def _():
                remote(
                    partial,
                    partials.at[z],
                    sum_send,
                    sum_recv,
                    i * PLACES + place,
                    y,
                ).start()


    @pl.when(points)
    def _():
        wait_bytes(branch_rows.at[0], branch_recv)
        wait_bytes(branch_rows.at[0], here_sem.at[5])

    @pl.when(rests)
    def _():
        wait_bytes(branch_rows, branch_recv)

    for row in range(2):
        added = f_rows[:, row].reshape(LOCAL, W).astype(F32) + branch_rows[row].astype(F32)
        out_rows[row] = added.astype(BF16)
    store_out = pltpu.make_async_copy(out_rows, out_hbm, here_sem.at[6])
    store_out.start()

    store_out.wait()

    @pl.when(works)
    def _():
        for which, tall in enumerate((tall_s, tall_f)):
            wait_bytes(tall.at[pl.ds(0, 10)], rows_send.at[which])
            for m, (step, here, there, rows) in enumerate(moves):

                @pl.when(inside(step))
                def _(m=m, tall=tall, which=which, here=here, rows=rows):
                    wait_bytes(tall.at[pl.ds(here, rows)], halo_send.at[which, m])

        @pl.when(points)
        def _():
            wait_bytes(mixed.at[pl.ds(0, ROWS - 1)], mix_send)
            wait_bytes(grad_cells.at[pl.ds(0, C // GROUP - 1)], back_send)

        @pl.when(rests)
        def _():
            wait_bytes(mixed, mix_send)


    @pl.when(idles)
    def _():
        for which, tall in enumerate((tall_s, tall_f)):
            wait_bytes(tall.at[pl.ds(0, 12)], rows_send.at[which])

        @pl.when(points)
        def _():
            wait_bytes(grad_cells, back_send)

    @pl.when(points)
    def _():
        wait_bytes(cell_grads.at[0], cot_send)
        wait_bytes(branch_cells.at[pl.ds(0, COUNT_Y - 1)], branch_send)

    @pl.when(rests)
    def _():
        wait_bytes(cell_grads.at[pl.ds(0, 2)], cot_send)

    @pl.when(works)
    def _():
        wait_bytes(partials.at[pl.ds(0, LEVELS - 1)], sum_recv)
        grads = jnp.sum(partials[...].astype(F32), axis=0)
        squares = jnp.sum(grads * grads, axis=1, keepdims=True) / (2 * K)
        steps = STEP_SIZE * grads * lax.rsqrt(squares + EPSILON)
        update[...] = steps.astype(BF16)
        pltpu.make_async_copy(update, updates.at[place], here_sem.at[7]).start()

        @loop(PLACES)
        def _(i):
            @pl.when(i != place)
            def _():
                remote(
                    update,
                    updates.at[place],
                    all_send,
                    all_recv,
                    level + i,
                    y,
                ).start()

        wait_bytes(partials.at[pl.ds(0, LEVELS - 1)], sum_send)
        wait_bytes(update, here_sem.at[7])
        wait_bytes(updates.at[pl.ds(0, PLACES - 1)], all_send)
        wait_bytes(updates.at[pl.ds(0, GROUPS - 1)], all_recv)

    @pl.when(idles)
    def _():
        wait_bytes(updates.at[pl.ds(0, GROUPS)], all_recv)


def finish(
    out_rows, step_ref, h_ref, v_ref, h_avg, v_avg, out_ref, h_new, v_new, h_swa, v_swa
):
    for row in range(2):
        out_ref[:, row, :] = out_rows[row]
    row = lax.broadcasted_iota(jnp.int32, (W, W), 0)
    lane = lax.broadcasted_iota(jnp.int32, (W, W), 1)
    from_v = jnp.logical_and(row < K, lane == row + 32)
    from_h = jnp.logical_and(row >= 64, lane == (214 - row) % W)
    order = jnp.logical_or(from_v, from_h).astype(F32).astype(BF16)
    steps = lax.dot_general(
        order,
        step_ref[...].reshape(W, W),
        (((1,), (1,)), ((), ())),
        preferred_element_type=F32,
    )
    new = h_ref[...] - steps[64 : 64 + K, 0:LOCAL]
    h_new[...] = new
    h_swa[...] = (AVERAGED * h_avg[...] + new) / (AVERAGED + 1)
    new = v_ref[...] - steps[0:K, 0:LOCAL]
    v_new[...] = new
    v_swa[...] = (AVERAGED * v_avg[...] + new) / (AVERAGED + 1)


def local(
    features,
    h_kernel,
    v_kernel,
    h_kernel_avg,
    v_kernel_avg,
    norm_gain,
    w_in,
    w_out,
    cotangent,
    tissue,
):
    vmem = pl.BlockSpec(memory_space=pltpu.VMEM)
    hbm = pl.BlockSpec(memory_space=pl.ANY)
    dma = pltpu.SemaphoreType.DMA
    out, step = pl.pallas_call(
        kernel,
        name="swa_step",
        out_shape=(
            jax.ShapeDtypeStruct((2, LOCAL, W), BF16),
            jax.ShapeDtypeStruct((PLACES, GROUP, W), BF16),
        ),
        in_specs=[hbm] * 8,
        out_specs=(hbm, hbm),
        scratch_shapes=[
            pltpu.VMEM((2, W), jnp.int32),
            pltpu.VMEM((K, LOCAL), F32),
            pltpu.VMEM((K, LOCAL), F32),
            pltpu.VMEM((C // W, W), F32),
            pltpu.VMEM((2, LOCAL, W), BF16),
            pltpu.VMEM((LOCAL, 2, W), BF16),
            pltpu.VMEM((LOCAL, 2, W), BF16),
            pltpu.VMEM((GROUPS, 2, GROUP, W), BF16),
            pltpu.VMEM((2, LOCAL, W), BF16),
            pltpu.VMEM((C, HID), BF16),
            pltpu.VMEM((HID, C), BF16),
            pltpu.VMEM((HID, C), BF16),
            pltpu.VMEM((C, HID), BF16),
            pltpu.VMEM((C, W), F32),
            pltpu.VMEM((W, W), F32),
            pltpu.VMEM((2, W + 2 * HALO, W), F32),
            pltpu.VMEM((GROUPS, 2, GROUP, W), BF16),
            pltpu.VMEM((TALL, GROUP, W), BF16),
            pltpu.VMEM((TALL, GROUP, W), BF16),
            pltpu.VMEM((TALL, GROUP, W), F32),
            pltpu.VMEM((ROWS * GROUP, TALL * GROUP), BF16),
            pltpu.VMEM((GROUP * W, ROWS * GROUP), BF16),
            pltpu.VMEM((K, GROUP, W), F32),
            pltpu.VMEM((ROWS, GROUP, W), BF16),
            pltpu.VMEM((COUNT_Y, LOCAL, W), BF16),
            pltpu.VMEM((HID, W), F32),
            pltpu.VMEM((C // GROUP, GROUP, W), BF16),
            pltpu.VMEM((C, W), F32),
            pltpu.VMEM((1, W), F32),
            pltpu.VMEM((C, W), BF16),
            pltpu.VMEM((HID, W), BF16),
            pltpu.VMEM((HID, W), BF16),
            pltpu.VMEM((C // GROUP, GROUP, W), BF16),
            pltpu.VMEM((ROWS, GROUP, W), BF16),
            pltpu.VMEM((COUNT_Y, LOCAL, W), BF16),
            pltpu.VMEM((2, LOCAL, W), BF16),
            pltpu.VMEM((GROUP, W), BF16),
            pltpu.VMEM((LEVELS, GROUP, W), BF16),
            pltpu.VMEM((GROUP, W), BF16),
            pltpu.SemaphoreType.REGULAR((3,)),
            dma((8,)),
            dma((8,)),
            dma((2,)),
            dma((PLACES + 1,)),
            dma((2, 4)),
            dma((2, 4)),
            dma,
            dma,
            dma,
            dma,
            dma,
            dma((4,)),
            dma,
            dma,
            dma,
            dma,
            dma,
            dma,
        ],
        compiler_params=pltpu.CompilerParams(collective_id=0, has_side_effects=True),
    )(
        features,
        cotangent,
        tissue,
        h_kernel.T,
        v_kernel.T,
        norm_gain.reshape(C // W, W),
        w_in,
        w_out,
    )
    taps = jax.ShapeDtypeStruct((K, LOCAL), F32)
    block_out, h_new, v_new, h_swa, v_swa = pl.pallas_call(
        finish,
        name="finish",
        out_shape=(jax.ShapeDtypeStruct((LOCAL, 2, W), BF16), taps, taps, taps, taps),
        in_specs=[vmem] * 6,
        out_specs=(vmem,) * 5,
    )(out, step, h_kernel.T, v_kernel.T, h_kernel_avg.T, v_kernel_avg.T)
    return (block_out, h_new.T, v_new.T, h_swa.T, v_swa.T)


def solution(mesh):
    return jax.shard_map(
        local,
        mesh=mesh,
        in_specs=(
            P("chan", "band", None),
            P("chan", None),
            P("chan", None),
            P("chan", None),
            P("chan", None),
            P(),
            P(),
            P(),
            P("chan", "band", None),
            P("band", None),
        ),
        out_specs=(
            P("chan", "band", None),
            P("chan", None),
            P("chan", None),
            P("chan", None),
            P("chan", None),
        ),
        check_vma=False,
    )
```
